128 devices in a mesh: ang: 8 (over x, core), det: 16 (over z, y).
Axes of the slice: x: 4, y: 4, z: 4, core: 2. Of those that a mesh axis runs over, the one named last changes fastest.
Arguments:
- raw_counts: float32 [256, 128, 4096], P('ang', None, 'det'), may hold values from 0.15 to 0.9
- dark_field: float32 [128, 4096], P(None, 'det'), may hold values from 0 to 0.1
- flat_field: float32 [128, 4096], P(None, 'det'), may hold values from 0.8 to 1.2
- destinations: int32 [32, 1], replicated, may hold values from 0 to 15; in each aligned block of 32 rows (0 to 31, 32 to 63, ...) at most 4 rows name the same one
- band_offsets: int32 [4096], replicated, may hold values from 0 to 4092, as said below
- band_weights: float32 [4, 4096], replicated, may hold values from 0.05 to 0.5
Outputs:
- parallel_slabs: float32 [256, 64, 4, 4096], P('ang', 'det')
The draws below stay inside these ranges and needn't reach their ends.
Inputs may be any that keep to these rules, and one draw needn't show every extreme that they name: `destinations`: no z-slab owner receives more than 4 row blocks, and some owner receives exactly 4. band_offsets[t] lies between t - 8 and t + 5.
All inputs are finite; a program needn't handle non-finite values.
Results may differ from the reference program's by a relative error of at most 0.0001.
Values sent between devices are 32-bit elements; how exact they have to be, the bound alone decides.
A program may use at most 64 MiB of HBM per device.

```python
import math
import jax
import jax.numpy as jnp
import numpy as np

RB = 4
SMW = 4
ITERS = 3
HB = 8
BW = 4
ANGLES = 256
NBLK = 32
ROWS = 128
COLS = 4096
MOST = 4
N_DET = 16


def draw_band_offsets(key, part):
    columns = jnp.arange(COLS, dtype=jnp.int32)
    jitter = jax.random.randint(key, (COLS,), -HB, HB - BW + 2, dtype=jnp.int32)
    offsets = jnp.clip(columns + jitter, 0, COLS - BW)
    offsets = jnp.where(columns == 0, 0, offsets)
    offsets = jnp.where(columns == COLS - 1, COLS - BW, offsets)
    return offsets.astype(jnp.int32)


def shard_levels(stream_key, shape, shards, low, largest):
    level = 1.0
    for dim, shards_of in shards:
        heights = jax.random.uniform(jax.random.fold_in(jax.random.fold_in(stream_key, 6), dim), (shards_of,), jnp.float32, low / len(shards), largest / len(shards))
        level = level * jnp.repeat(jnp.exp(heights), shape[dim] // shards_of).reshape((-1,) + (1,) * (len(shape) - 1 - dim))
    return level


def deal_out(key, own, number, rows, number_of, top, limit, skew):
    sequence = jax.random.permutation(key, number_of)
    packed, common = load_shares(number_of, rows * top, limit, skew, True), load_shares(number_of, rows * top, limit, skew, False)
    places = jnp.arange(number_of)

    def named(lengths, rotation):
        used = int((lengths > 0).sum())
        fixed = max(1, used // 4)
        passed = fixed + (places - fixed + rotation * (used - fixed)) % max(1, number_of - fixed)
        return jnp.zeros((number_of,), jnp.int32).at[sequence[jnp.where(places < fixed, places, passed)]].set(jnp.asarray(lengths, jnp.int32))

    lengths = jnp.where(number % 4 == 0, named(packed, number // 4), named(common, number - number // 4 - 1))
    mixed = jax.random.permutation(jax.random.fold_in(own, 3), number_of)
    source_of, sink = mixed[0:number_of // 2 * 2:2], mixed[1:number_of // 2 * 2:2]
    slack = jnp.minimum(lengths[source_of] - 1, limit - lengths[sink]) // 2
    slack = jnp.where((source_of == sequence[0]) | (sink == sequence[0]) | (lengths[sink] == 0), 0, jnp.maximum(slack, 0))
    passed = jax.random.randint(jax.random.fold_in(own, 4), (number_of // 2,), 0, 1 << 20) % (slack + 1)
    lengths = lengths.at[source_of].add(-passed).at[sink].add(passed)
    members = jnp.searchsorted(jnp.cumsum(lengths), jnp.arange(rows * top), side="right").astype(jnp.int32)
    listing = members.reshape(top, rows).T
    listing = listing[jax.random.permutation(jax.random.fold_in(own, 1), rows)]
    rotation = jax.random.randint(jax.random.fold_in(own, 2), (rows, 1), 0, top)
    return jnp.take_along_axis(listing, (jnp.arange(top)[None, :] + rotation) % top, axis=1)


def load_shares(number_of, total, reach, slope, full):
    weights = [(1 << 20) // math.isqrt(grade ** slope) + 1 for grade in range(1, number_of + 1)]
    largest = reach if full else min(reach, max(-(-total // number_of), total * weights[0] // sum(weights)))
    least = 1 if total - largest >= number_of - 1 else 0
    given, surplus = [largest] + [least] * (number_of - 1), total - largest - least * (number_of - 1)
    while surplus > 0:
        candidates = [i for i in range(1, number_of) if given[i] < largest] or [i for i in range(1, number_of) if given[i] < reach]
        mass, remaining = sum([weights[i] for i in candidates]), surplus
        for i in candidates:
            addition = min(reach - given[i], max(1, remaining * weights[i] // mass), surplus)
            given[i] = given[i] + addition
            surplus = surplus - addition
    return np.array(given)


def setup_inputs(seed: int = 0) -> dict:
    key_list = jax.random.split(jax.random.key(seed), 7)
    raw_counts = jnp.clip(0.15 + 0.75 * jax.random.uniform(key_list[0], (ANGLES, ROWS, COLS), jnp.float32) ** shard_levels(key_list[0], (ANGLES, ROWS, COLS), ((0, 8), (2, 16)), -0.2, 0.2), 0.15, 0.9)
    dark_field = jnp.clip(0.1 * jax.random.uniform(key_list[1], (ROWS, COLS), jnp.float32) ** shard_levels(key_list[1], (ROWS, COLS), ((1, 16),), -0.2, 0.2), 0.0, 0.1)
    flat_field = jnp.clip(0.8 + 0.40000004 * jax.random.uniform(key_list[2], (ROWS, COLS), jnp.float32) ** shard_levels(key_list[2], (ROWS, COLS), ((1, 16),), -0.2, 0.2), 0.8, 1.2)
    destinations_keys = jax.random.split(jax.random.fold_in(key_list[3], 1), NBLK // NBLK)
    destinations_turns = jax.random.permutation(jax.random.fold_in(key_list[3], 3), NBLK // NBLK)
    destinations = jax.vmap(lambda own, number: deal_out(jax.random.fold_in(key_list[3], 2), own, number, NBLK, N_DET, 1, MOST, 2))(destinations_keys, destinations_turns).reshape((NBLK, 1))
    band_offsets = draw_band_offsets(jax.random.fold_in(key_list[6], 71), 0)
    band_weights = jnp.clip(jnp.exp(jax.random.uniform(key_list[5], (BW, COLS), jnp.float32, math.log(0.05), math.log(0.5))), 0.05, 0.5)
    return dict(raw_counts=raw_counts, dark_field=dark_field, flat_field=flat_field, destinations=destinations, band_offsets=band_offsets, band_weights=band_weights)


cauchy_scale = 0.2


def smooth_rows(values):
    padded = jnp.pad(values, ((0, 0), (0, 0), (SMW, SMW)))
    summed = padded[:, :, 0:COLS]
    for position in range(1, 2 * SMW + 1):
        summed = summed + padded[:, :, position:position + COLS]
    columns = jnp.arange(COLS, dtype=jnp.int32)
    counts = jnp.minimum(columns + SMW, COLS - 1) - jnp.maximum(columns - SMW, 0) + 1
    return summed / counts.astype(jnp.float32)


def rebin(values, offsets, weights):
    summed = weights[0] * jnp.take(values, offsets, axis=-1)
    for position in range(1, BW):
        summed = summed + weights[position] * jnp.take(values, offsets + position, axis=-1)
    return summed


def slot_tables(destinations, owners, most):
    targets = destinations[:, 0]
    block_ids = jnp.arange(targets.shape[0], dtype=jnp.int32)
    same_earlier = (targets[:, None] == targets[None, :]) & (block_ids[None, :] < block_ids[:, None])
    slot_rank = jnp.sum(same_earlier.astype(jnp.int32), axis=1)
    owner_ids = jnp.arange(owners, dtype=jnp.int32)
    rank_ids = jnp.arange(most, dtype=jnp.int32)
    matching = ((targets[None, None, :] == owner_ids[:, None, None]) & (slot_rank[None, None, :] == rank_ids[None, :, None])).astype(jnp.int32)
    chosen = jnp.sum(matching * block_ids[None, None, :], axis=2)
    filled = jnp.sum(matching, axis=2)
    return chosen, filled


def reference(raw_counts, dark_field, flat_field, destinations, band_offsets, band_weights):
    projected = -jnp.log((raw_counts - dark_field) / (flat_field - dark_field))
    detail = projected - smooth_rows(projected)
    gain_map = jnp.sum(detail, axis=0) / ANGLES
    for reweight_pass in range(ITERS):
        scaled = (detail - gain_map) / cauchy_scale
        weights = 1.0 / (1.0 + scaled * scaled)
        gain_map = jnp.sum(weights * detail, axis=0) / jnp.sum(weights, axis=0)
    corrected = projected - gain_map
    rebinned = rebin(corrected, band_offsets, band_weights)
    blocks = rebinned.reshape(ANGLES, NBLK, RB, COLS)
    chosen, filled = slot_tables(destinations, N_DET, MOST)
    picked = jnp.take(blocks, chosen.reshape(-1), axis=1)
    return picked * filled.reshape(-1)[None, :, None, None].astype(jnp.float32)
```

```python
import functools

import jax
import jax.numpy as jnp
from jax import lax
from jax.experimental import pallas as pl
from jax.experimental.pallas import tpu as pltpu
from jax.sharding import PartitionSpec as P

RB = 4
SMW = 4
ITERS = 3
BW = 4
MOST = 4
NBLK = 32
NDET = 16
SIDE = 4
W = 256
COLS = NDET * W
CAPS = (16,)
MESH = pl.DeviceIdType.MESH
F32 = jnp.float32
BF16 = jnp.bfloat16


def halves(x):
    high = x.astype(BF16)
    return high, (x - high.astype(F32)).astype(BF16)


def tables(destinations, cap):
    target = destinations[:, 0]
    ids = jnp.arange(NBLK, dtype=jnp.int32)
    earlier = ids[None, :] < ids[:, None]

    def rank(key):
        return jnp.sum(((key[:, None] == key[None, :]) & earlier).astype(jnp.int32), axis=1)

    def listed(key, place, groups, size):
        match = (key[None, None, :] == jnp.arange(groups, dtype=jnp.int32)[:, None, None]) & (
            place[None, None, :] == jnp.arange(size, dtype=jnp.int32)[None, :, None]
        )
        return match.astype(jnp.int32)

    zt, yt = target // SIDE, target % SIDE
    zr, yr = rank(zt), rank(yt)
    slot = listed(target, rank(target), NDET, MOST)

    def pick(match, values):
        return jnp.sum(match * values[None, None, :], axis=2).reshape(-1)

    chosen = pick(slot, ids)
    filled = jnp.sum(slot, axis=2).reshape(-1)
    return (
        chosen,
        pick(slot, zr),
        pick(slot, yr),
        pick(listed(zt, zr, SIDE, cap), ids),
        pick(listed(yt, yr, SIDE, cap), ids),
        filled,
    )


def move_kernel(cap, chosen, zpos, ypos, zlist, ylist, raw_hbm, dark, flat, slabs, gains, *scr):
    (raw, vals, det, gmap, sa, sb, ra1, ra2, ra3, rb1, rb2, rb3, ta, tb, halo_out, halo_in, edge, part,
     got, final, gslot, raw_sem, s1, r1, s2, r2, loc, hs, hr, xs, xr, ys, yr, gs, gr) = scr
    ra, rb = (None, ra1, ra2, ra3), (None, rb1, rb2, rb3)
    me = lax.axis_index("det")
    ang = lax.axis_index("ang")
    z, y = me // SIDE, me % SIDE

    def at(dz, dy):
        return lax.rem(z + dz, SIDE) * SIDE + lax.rem(y + dy, SIDE)

    def to_det(src, dst, send, recv, where):
        return pltpu.make_async_remote_copy(src, dst, send, recv, device_id={"det": where}, device_id_type=MESH)

    def to_ang(src, dst, send, recv, where):
        return pltpu.make_async_remote_copy(src, dst, send, recv, device_id={"ang": where}, device_id_type=MESH)

    loads = [pltpu.make_async_copy(raw_hbm.at[pl.ds(16 * h, 16)], raw.at[h], raw_sem.at[h]) for h in range(2)]
    for cp in loads:
        cp.start()
    bar = pltpu.get_barrier_semaphore()
    for p in range(1, NDET):
        pl.semaphore_signal(bar, inc=1, device_id={"det": lax.rem(me + p, NDET)}, device_id_type=MESH)
    for p in range(1, 8):
        pl.semaphore_signal(bar, inc=1, device_id={"ang": lax.rem(ang + p, 8)}, device_id_type=MESH)

    low = lax.broadcasted_iota(jnp.int32, (8, W), 0) < RB
    lane = lax.broadcasted_iota(jnp.int32, (8, 128), 1)

    def project(h):
        @pl.loop(0, 16)
        def _(q):
            rows = pl.ds(pl.multiple_of(8 * q, 8), 8)
            d = dark[rows, :]
            x = -jnp.log((raw[h, :, rows, :] - d) / (flat[rows, :] - d))
            x = x.reshape(8, 2, 8, W)
            for p in range(8):
                x0, x1 = x[p, 0], x[p, 1]
                vals[2 * q, h, p] = jnp.where(low, x0, pltpu.roll(x1, RB, 0))
                vals[2 * q + 1, h, p] = jnp.where(low, pltpu.roll(x0, RB, 0), x1)

    def pack(h):
        @pl.loop(0, 8)
        def _(g):
            right = jnp.zeros((8, 128), F32)
            left = jnp.zeros((8, 128), F32)
            for i in range(32):
                x = vals[4 * g + i // 8, h, i % 8]
                here = (lane >= 4 * i) & (lane < 4 * i + 4)
                right = jnp.where(here, pltpu.roll(x[:, 128:], (4 * i + 4) % 128, 1), right)
                left = jnp.where(here, pltpu.roll(x[:, :128], 4 * i, 1), left)
            halo_out[h, 0, g] = right
            halo_out[h, 1, g] = left

    halos = []
    first = []
    second = []
    stay = []

    def halo(h):
        for side, where in ((0, lax.rem(me + 1, NDET)), (1, lax.rem(me + NDET - 1, NDET))):
            cp = to_det(halo_out.at[h, side], halo_in.at[h, side], hs.at[h, side], hr.at[h, side], where)
            cp.start()
            halos.append(cp)

    def first_hop(h):
        listing, out, into = (zlist, sa, ra) if h == 0 else (ylist, sb, rb)
        for d in (1, 3, 2):
            group = lax.rem((z if h == 0 else y) + d, SIDE)

            @pl.loop(0, cap)
            def _(c):
                out[d - 1, c] = vals[listing[group * cap + c], h]

            where = at(d, 0) if h == 0 else at(0, d)
            cp = to_det(out.at[d - 1], into[d], s1.at[h, d], r1.at[h, d], where)
            cp.start()
            first.append((h, d, cp))

    def second_hop(h, d):
        out = ta if h == 0 else tb
        col = at(SIDE - d, 0) if h == 0 else at(0, SIDE - d)
        for e in (1, 3, 2, 0):
            owner = at(0, e) if h == 0 else at(e, 0)
            for j in range(MOST):
                if d == 0:
                    out[d, e, j] = vals[chosen[owner * MOST + j], h]
                elif h == 0:
                    out[d, e, j] = ra[d][zpos[owner * MOST + j]]
                else:
                    out[d, e, j] = rb[d][ypos[owner * MOST + j]]
            if e == 0:
                cp = pltpu.make_async_copy(out.at[d, e], slabs.at[col, h], loc.at[h, d])
                stay.append(cp)
            else:
                cp = to_det(out.at[d, e], slabs.at[col, h], s2.at[h, d, e], r2.at[h, d, e], owner)
                second.append(cp)
            cp.start()

    def arrived(h, dist):
        for hh, d, cp in first:
            if hh == h and d == dist:
                cp.wait_recv()

    loads[0].wait()
    project(0)
    pack(0)
    pl.semaphore_wait(bar, NDET - 1 + 7)
    halo(0)
    first_hop(0)
    loads[1].wait()
    project(1)
    pack(1)
    halo(1)
    first_hop(1)
    second_hop(0, 0)
    second_hop(1, 0)

    src = lax.broadcasted_iota(jnp.int32, (W, W), 0)
    dst = lax.broadcasted_iota(jnp.int32, (W, W), 1)
    band = (jnp.abs(src - dst) <= SMW).astype(BF16)
    erow = lax.broadcasted_iota(jnp.int32, (128, W), 0)
    ecol = lax.broadcasted_iota(jnp.int32, (128, W), 1)
    at_left = (erow < 4) & (ecol <= erow)
    at_right = (erow >= 4) & (erow < 8) & (W + (erow - 4) - ecol <= SMW)
    eband = (at_left | at_right).astype(BF16)
    col = me * W + lax.broadcasted_iota(jnp.int32, (8, W), 1)
    number = jnp.minimum(col + SMW, COLS - 1) - jnp.maximum(col - SMW, 0) + 1
    share = (1.0 / number.astype(F32))[None]
    for cp in halos:
        cp.wait_recv()
    for h in range(2):
        @pl.loop(0, 8)
        def _(g):
            before = jnp.where(me == 0, 0.0, halo_in[h, 0, g])
            after = jnp.where(me == NDET - 1, 0.0, halo_in[h, 1, g])
            for i in range(32):
                a = pltpu.roll(before, (128 - 4 * i) % 128, 1)
                b = pltpu.roll(after, (132 - 4 * i) % 128, 1)
                edge[i] = jnp.where(lane < 4, a, jnp.where(lane < 8, b, 0.0))
            x = jnp.concatenate([vals[4 * g + i, h] for i in range(4)], axis=0)
            xh, xl = halves(x.reshape(256, W))
            eh, el = halves(edge[...].reshape(256, 128))
            summed = (
                jnp.dot(xh, band, preferred_element_type=F32)
                + jnp.dot(xl, band, preferred_element_type=F32)
                + jnp.dot(eh, eband, preferred_element_type=F32)
                + jnp.dot(el, eband, preferred_element_type=F32)
            )
            detail = x - summed.reshape(32, 8, W) * share
            for i in range(4):
                det[4 * g + i, h] = detail[8 * i : 8 * i + 8]

    def both(s):
        return s + pltpu.roll(s, RB, 0)

    def reduce_all(step):
        sends = []
        for p in range(1, 8):
            peer = lax.rem(ang + p, 8)
            cp = to_ang(part.at[step, peer], got.at[step, p], xs.at[step, p], xr.at[step, p], peer)
            cp.start()
            sends.append(cp)
        for cp in sends:
            cp.wait_recv()
        for t in range(2):
            num = part[step, ang, 0, t]
            den = part[step, ang, 1, t]
            for p in range(1, 8):
                num = num + got[step, p, 0, t]
                den = den + got[step, p, 1, t]
            final[step, ang, t] = num / den
        gathers = []
        for p in range(1, 8):
            peer = lax.rem(ang + p, 8)
            cp = to_ang(final.at[step, ang], final.at[step, ang], ys.at[step, p], yr.at[step, p], peer)
            cp.start()
            gathers.append(cp)
        for p in range(1, 8):
            gathers[p - 1].wait_recv()

        @pl.loop(0, 8)
        def _(m):
            for t in range(2):
                tile = final[step, m, t]
                turned = pltpu.roll(tile, RB, 0)
                gmap[4 * m + 2 * t] = jnp.where(low, tile, turned)
                gmap[4 * m + 2 * t + 1] = jnp.where(low, turned, tile)

        return sends + gathers

    pending = []

    @pl.loop(0, 8)
    def _(m):
        for t in range(2):
            sums = []
            for b in range(2):
                block = 4 * m + 2 * t + b
                sums.append(both(jnp.sum(det[block, 0], axis=0) + jnp.sum(det[block, 1], axis=0)))
            part[0, m, 0, t] = jnp.where(low, sums[0], sums[1])
            part[0, m, 1, t] = jnp.full((8, W), 32.0, F32)

    pending += reduce_all(0)
    for step in range(1, ITERS + 1):
        @pl.loop(0, 8)
        def _(m):
            for t in range(2):
                nums, dens = [], []
                for b in range(2):
                    block = 4 * m + 2 * t + b
                    gain = gmap[block][None]
                    num = jnp.zeros((8, W), F32)
                    den = jnp.zeros((8, W), F32)
                    for h in range(2):
                        d = det[block, h]
                        scaled = (d - gain) / 0.2
                        weight = 1.0 / (1.0 + scaled * scaled)
                        num = num + jnp.sum(weight * d, axis=0)
                        den = den + jnp.sum(weight, axis=0)
                    nums.append(both(num))
                    dens.append(both(den))
                part[step, m, 0, t] = jnp.where(low, nums[0], nums[1])
                part[step, m, 1, t] = jnp.where(low, dens[0], dens[1])

        pending += reduce_all(step)
        if step < ITERS:
            for d in (1, 3, 2)[0 : 2] if step == 1 else (2,):
                for h in range(2):
                    arrived(h, d)
                    second_hop(h, d)

    give = []
    for p in range(NDET):
        owner = lax.rem(me + p, NDET)
        for t in range(2):
            a = gmap[chosen[owner * MOST + 2 * t]]
            b = gmap[chosen[owner * MOST + 2 * t + 1]]
            gslot[p, t] = jnp.where(low, a, b)
        if p == 0:
            cp = pltpu.make_async_copy(gslot.at[p], gains.at[me], gs.at[p])
            stay.append(cp)
        else:
            cp = to_det(gslot.at[p], gains.at[me], gs.at[p], gr.at[p], owner)
            give.append(cp)
        cp.start()

    for cp in give + second:
        cp.wait_recv()
    for cp in stay:
        cp.wait()
    for cp in give + second + halos + pending + [c for _, _, c in first]:
        cp.wait_send()


def move(cap, chosen, zpos, ypos, zlist, ylist, raw, dark, flat):
    chunk = (8, 8, W)
    dma = pltpu.SemaphoreType.DMA
    scratch = [
        pltpu.VMEM((2, 16, 128, W), F32),
        pltpu.VMEM((NBLK, 2) + chunk, F32),
        pltpu.VMEM((NBLK, 2) + chunk, F32),
        pltpu.VMEM((NBLK, 8, W), F32),
        pltpu.VMEM((3, cap) + chunk, F32),
        pltpu.VMEM((3, cap) + chunk, F32),
    ]
    scratch += [pltpu.VMEM((cap,) + chunk, F32) for _ in range(6)]
    scratch += [
        pltpu.VMEM((4, 4, MOST) + chunk, F32),
        pltpu.VMEM((4, 4, MOST) + chunk, F32),
        pltpu.VMEM((2, 2, 8, 8, 128), F32),
        pltpu.VMEM((2, 2, 8, 8, 128), F32),
        pltpu.VMEM((32, 8, 128), F32),
        pltpu.VMEM((ITERS + 1, 8, 2, 2, 8, W), F32),
        pltpu.VMEM((ITERS + 1, 8, 2, 2, 8, W), F32),
        pltpu.VMEM((ITERS + 1, 8, 2, 8, W), F32),
        pltpu.VMEM((NDET, 2, 8, W), F32),
        dma((2,)),
        dma((2, 4)), dma((2, 4)),
        dma((2, 4, 4)), dma((2, 4, 4)),
        dma((2, 4)),
        dma((2, 2)), dma((2, 2)),
        dma((ITERS + 1, 8)), dma((ITERS + 1, 8)), dma((ITERS + 1, 8)), dma((ITERS + 1, 8)),
        dma((NDET,)), dma((NDET,)),
    ]
    smem = pl.BlockSpec(memory_space=pltpu.SMEM)
    vmem = pl.BlockSpec(memory_space=pltpu.VMEM)
    hbm = pl.BlockSpec(memory_space=pl.ANY)
    return pl.pallas_call(
        functools.partial(move_kernel, cap),
        out_shape=(
            jax.ShapeDtypeStruct((NDET, 2, MOST) + chunk, F32),
            jax.ShapeDtypeStruct((NDET, 2, 8, W), F32),
        ),
        in_specs=[smem] * 5 + [hbm, vmem, vmem],
        out_specs=(hbm, hbm),
        scratch_shapes=scratch,
        compiler_params=pltpu.CompilerParams(
            collective_id=cap, has_side_effects=True, vmem_limit_bytes=56 * 2**20
        ),
        name=f"move{cap}",
    )(chosen, zpos, ypos, zlist, ylist, raw, dark, flat)


def rebin_kernel(filled, slabs_hbm, gains, offsets, weights, out, slabs, xh, xl, eh, el, sems):
    c = pl.program_id(0)
    me = lax.axis_index("det")

    def load(i):
        return pltpu.make_async_copy(slabs_hbm.at[i], slabs.at[i], sems.at[i])

    @pl.when(c == 0)
    def _():
        @pl.loop(0, NDET)
        def _(i):
            load(i).start()

        load(0).wait()

    @pl.when(c < NDET - 1)
    def _():
        load(c + 1).wait()

    rel = offsets[...] - c * W
    wts = weights[...]
    row = lax.broadcasted_iota(jnp.int32, (W, W), 0)

    def coefficients(place):
        total = jnp.zeros((W, W), F32)
        for k in range(BW):
            total = jnp.where(place == rel + k, wts[k : k + 1], total)
        return halves(total)

    mh, ml = coefficients(row)
    lh, ll = coefficients(jnp.where(row < 128, row - 128, row + 128))
    low = lax.broadcasted_iota(jnp.int32, (8, W), 0) < RB
    before = jnp.maximum(c - 1, 0)
    after = jnp.minimum(c + 1, NDET - 1)

    def gain(chunk, j):
        tile = gains[chunk, j // 2]
        turned = pltpu.roll(tile, RB, 0)
        return jnp.where(low, tile, turned) if j % 2 == 0 else jnp.where(low, turned, tile)

    for j in range(MOST):
        on = filled[me * MOST + j].astype(F32)
        g = gain(c, j) * on
        gl = gain(before, j)[:, 128:] * on
        gr = gain(after, j)[:, :128] * on
        for h in range(2):
            rows = pl.ds((h * MOST + j) * 64, 64)
            x = slabs[c, h, j] * on - g[None]
            a, b = halves(x.reshape(64, W))
            xh[rows, :] = a
            xl[rows, :] = b
            a, b = halves((slabs[before, h, j, :, :, 128:] * on - gl[None]).reshape(64, 128))
            eh[rows, :128] = a
            el[rows, :128] = b
            a, b = halves((slabs[after, h, j, :, :, :128] * on - gr[None]).reshape(64, 128))
            eh[rows, 128:] = a
            el[rows, 128:] = b
    acc = (
        jnp.dot(xh[...], mh, preferred_element_type=F32)
        + jnp.dot(xl[...], mh, preferred_element_type=F32)
        + jnp.dot(xh[...], ml, preferred_element_type=F32)
        + jnp.dot(eh[...], lh, preferred_element_type=F32)
        + jnp.dot(el[...], lh, preferred_element_type=F32)
        + jnp.dot(eh[...], ll, preferred_element_type=F32)
    )
    for h in range(2):
        for j in range(MOST):
            i = (h * MOST + j) * 64
            out[16 * h : 16 * h + 16, j] = acc[i : i + 64].reshape(16, RB, W)


def rebin(filled, slabs, gains, offsets, weights):
    return pl.pallas_call(
        rebin_kernel,
        grid=(NDET,),
        out_shape=jax.ShapeDtypeStruct((32, MOST, RB, COLS), F32),
        in_specs=[
            pl.BlockSpec(memory_space=pltpu.SMEM),
            pl.BlockSpec(memory_space=pl.ANY),
            pl.BlockSpec((NDET, 2, 8, W), lambda c: (0, 0, 0, 0)),
            pl.BlockSpec((1, W), lambda c: (0, c)),
            pl.BlockSpec((BW, W), lambda c: (0, c)),
        ],
        out_specs=pl.BlockSpec((32, MOST, RB, W), lambda c: (0, 0, 0, c)),
        scratch_shapes=[
            pltpu.VMEM((NDET, 2, MOST, 8, 8, W), F32),
            pltpu.VMEM((512, W), BF16),
            pltpu.VMEM((512, W), BF16),
            pltpu.VMEM((512, W), BF16),
            pltpu.VMEM((512, W), BF16),
            pltpu.SemaphoreType.DMA((NDET,)),
        ],
        compiler_params=pltpu.CompilerParams(vmem_limit_bytes=56 * 2**20),
        name="rebin",
    )(filled, slabs, gains, offsets.reshape(1, COLS), weights)


def body(raw_counts, dark_field, flat_field, destinations, band_offsets, band_weights):
    target = destinations[:, 0]
    if len(CAPS) == 1:
        *listing, filled = tables(destinations, CAPS[0])
        slabs, gains = move(CAPS[0], *listing, raw_counts, dark_field, flat_field)
    else:
        sides = jnp.concatenate([target // SIDE, SIDE + target % SIDE])
        load = jnp.max(jnp.sum((sides[:, None] == jnp.arange(2 * SIDE)[None, :]).astype(jnp.int32), axis=0))
        branch = sum((load > cap).astype(jnp.int32) for cap in CAPS[:-1])
        filled = tables(destinations, CAPS[-1])[-1]

        def with_cap(cap):
            return lambda dest, *arrays: move(cap, *tables(dest, cap)[:-1], *arrays)

        slabs, gains = lax.switch(
            branch, [with_cap(cap) for cap in CAPS], destinations, raw_counts, dark_field, flat_field
        )
    return rebin(filled, slabs, gains, band_offsets, band_weights)


def solution(mesh):
    placed = (P("ang", None, "det"), P(None, "det"), P(None, "det"), P(), P(), P())
    return jax.shard_map(
        body, mesh=mesh, in_specs=placed, out_specs=P("ang", "det", None, None), check_vma=False
    )
```

```python
import functools

import jax
import jax.numpy as jnp
from jax import lax
from jax.experimental import pallas as pl
from jax.experimental.pallas import tpu as pltpu
from jax.sharding import PartitionSpec as P

RB = 4
SMW = 4
ITERS = 3
BW = 4
MOST = 4
NBLK = 32
NDET = 16
SIDE = 4
W = 256
COLS = NDET * W
CAPS = (9, 10, 11, 16)
MESH = pl.DeviceIdType.MESH
F32 = jnp.float32
BF16 = jnp.bfloat16


def halves(x):
    high = x.astype(BF16)
    return high, (x - high.astype(F32)).astype(BF16)


CHOSEN, ZPOS, YPOS, FILLED, ZLIST, YLIST, PLAN = 0, 64, 128, 192, 256, 320, 384
LIST = 16


def plan_kernel(target, plan, branch, count):
    @pl.loop(0, PLAN // 16)
    def _(i):
        for k in range(16):
            plan[16 * i + k] = 0

    for k in range(NDET + 2 * SIDE):
        count[k] = 0

    @pl.loop(0, NBLK)
    def _(b):
        owner = target[b]
        zg = NDET + owner // SIDE
        yg = NDET + SIDE + owner % SIDE
        place, zp, yp = count[owner], count[zg], count[yg]
        count[owner] = place + 1
        count[zg] = zp + 1
        count[yg] = yp + 1
        slot = owner * MOST + place
        plan[CHOSEN + slot] = b
        plan[ZPOS + slot] = zp
        plan[YPOS + slot] = yp
        plan[FILLED + slot] = 1
        plan[ZLIST + (zg - NDET) * LIST + zp] = b
        plan[YLIST + (yg - NDET - SIDE) * LIST + yp] = b

    most = count[NDET]
    for k in range(1, 2 * SIDE):
        most = jnp.maximum(most, count[NDET + k])
    branch[0] = sum((most > cap).astype(jnp.int32) for cap in CAPS[:-1]) + jnp.int32(0)


def make_plan(destinations):
    smem = pl.BlockSpec(memory_space=pltpu.SMEM)
    return pl.pallas_call(
        plan_kernel,
        out_shape=(jax.ShapeDtypeStruct((PLAN,), jnp.int32), jax.ShapeDtypeStruct((1,), jnp.int32)),
        in_specs=[smem],
        out_specs=(smem, smem),
        scratch_shapes=[pltpu.SMEM((NDET + 2 * SIDE,), jnp.int32)],
        name="plan",
    )(destinations.reshape(NBLK))


def move_kernel(cap, plan, raw_hbm, dark, flat, slabs, gains, *scr):
    (raw, vals, det, gmap, sa, sb, ra1, ra2, ra3, rb1, rb2, rb3, ta, tb, halo_out, halo_in, edge, part,
     got, final, gslot, raw_sem, s1, r1, s2, r2, loc, hs, hr, xs, xr, ys, yr, gs, gr) = scr
    ra, rb = (None, ra1, ra2, ra3), (None, rb1, rb2, rb3)
    me = lax.axis_index("det")
    ang = lax.axis_index("ang")
    z, y = me // SIDE, me % SIDE

    def at(dz, dy):
        return lax.rem(z + dz, SIDE) * SIDE + lax.rem(y + dy, SIDE)

    def to_det(src, dst, send, recv, where):
        return pltpu.make_async_remote_copy(src, dst, send, recv, device_id={"det": where}, device_id_type=MESH)

    def to_ang(src, dst, send, recv, where):
        return pltpu.make_async_remote_copy(src, dst, send, recv, device_id={"ang": where}, device_id_type=MESH)

    loads = [pltpu.make_async_copy(raw_hbm.at[pl.ds(16 * h, 16)], raw.at[h], raw_sem.at[h]) for h in range(2)]
    for cp in loads:
        cp.start()
    bar = pltpu.get_barrier_semaphore()
    for p in range(1, NDET):
        pl.semaphore_signal(bar, inc=1, device_id={"det": lax.rem(me + p, NDET)}, device_id_type=MESH)
    for p in range(1, 8):
        pl.semaphore_signal(bar, inc=1, device_id={"ang": lax.rem(ang + p, 8)}, device_id_type=MESH)

    low = lax.broadcasted_iota(jnp.int32, (8, W), 0) < RB
    lane = lax.broadcasted_iota(jnp.int32, (8, 128), 1)

    def project(h):
        @pl.loop(0, 16)
        def _(q):
            rows = pl.ds(pl.multiple_of(8 * q, 8), 8)
            d = dark[rows, :]
            x = -jnp.log((raw[h, :, rows, :] - d) / (flat[rows, :] - d))
            x = x.reshape(8, 2, 8, W)
            for p in range(8):
                x0, x1 = x[p, 0], x[p, 1]
                vals[2 * q, h, p] = jnp.where(low, x0, pltpu.roll(x1, RB, 0))
                vals[2 * q + 1, h, p] = jnp.where(low, pltpu.roll(x0, RB, 0), x1)

    def pack(h):
        @pl.loop(0, 8)
        def _(g):
            right = jnp.zeros((8, 128), F32)
            left = jnp.zeros((8, 128), F32)
            for i in range(32):
                x = vals[4 * g + i // 8, h, i % 8]
                here = (lane >= 4 * i) & (lane < 4 * i + 4)
                right = jnp.where(here, pltpu.roll(x[:, 128:], (4 * i + 4) % 128, 1), right)
                left = jnp.where(here, pltpu.roll(x[:, :128], 4 * i, 1), left)
            halo_out[h, 0, g] = right
            halo_out[h, 1, g] = left

    halos = []
    first = []
    second = []
    stay = []

    def halo(h):
        for side, where in ((0, lax.rem(me + 1, NDET)), (1, lax.rem(me + NDET - 1, NDET))):
            cp = to_det(halo_out.at[h, side], halo_in.at[h, side], hs.at[h, side], hr.at[h, side], where)
            cp.start()
            halos.append(cp)

    def first_hop(h):
        listing, out, into = (ZLIST, sa, ra) if h == 0 else (YLIST, sb, rb)
        for d in (1, 3, 2):
            group = lax.rem((z if h == 0 else y) + d, SIDE)

            @pl.loop(0, cap)
            def _(c):
                out[d - 1, c] = vals[plan[listing + group * LIST + c], h]

            where = at(d, 0) if h == 0 else at(0, d)
            cp = to_det(out.at[d - 1], into[d], s1.at[h, d], r1.at[h, d], where)
            cp.start()
            first.append((h, d, cp))

    def second_hop(h, d):
        out = ta if h == 0 else tb
        col = at(SIDE - d, 0) if h == 0 else at(0, SIDE - d)
        for e in (1, 3, 2, 0):
            owner = at(0, e) if h == 0 else at(e, 0)
            for j in range(MOST):
                if d == 0:
                    out[d, e, j] = vals[plan[CHOSEN + owner * MOST + j], h]
                elif h == 0:
                    out[d, e, j] = ra[d][plan[ZPOS + owner * MOST + j]]
                else:
                    out[d, e, j] = rb[d][plan[YPOS + owner * MOST + j]]
            if e == 0:
                cp = pltpu.make_async_copy(out.at[d, e], slabs.at[col, h], loc.at[h, d])
                stay.append(cp)
            else:
                cp = to_det(out.at[d, e], slabs.at[col, h], s2.at[h, d, e], r2.at[h, d, e], owner)
                second.append(cp)
            cp.start()

    def arrived(h, dist):
        for hh, d, cp in first:
            if hh == h and d == dist:
                cp.wait_recv()

    loads[0].wait()
    project(0)
    pack(0)
    pl.semaphore_wait(bar, NDET - 1 + 7)
    halo(0)
    first_hop(0)
    loads[1].wait()
    project(1)
    pack(1)
    halo(1)
    first_hop(1)
    second_hop(0, 0)
    second_hop(1, 0)

    src = lax.broadcasted_iota(jnp.int32, (W, W), 0)
    dst = lax.broadcasted_iota(jnp.int32, (W, W), 1)
    band = (jnp.abs(src - dst) <= SMW).astype(BF16)
    erow = lax.broadcasted_iota(jnp.int32, (128, W), 0)
    ecol = lax.broadcasted_iota(jnp.int32, (128, W), 1)
    at_left = (erow < 4) & (ecol <= erow)
    at_right = (erow >= 4) & (erow < 8) & (W + (erow - 4) - ecol <= SMW)
    eband = (at_left | at_right).astype(BF16)
    col = me * W + lax.broadcasted_iota(jnp.int32, (8, W), 1)
    number = jnp.minimum(col + SMW, COLS - 1) - jnp.maximum(col - SMW, 0) + 1
    share = (1.0 / number.astype(F32))[None]
    for cp in halos:
        cp.wait_recv()
    for h in range(2):
        @pl.loop(0, 8)
        def _(g):
            before = jnp.where(me == 0, 0.0, halo_in[h, 0, g])
            after = jnp.where(me == NDET - 1, 0.0, halo_in[h, 1, g])
            for i in range(32):
                a = pltpu.roll(before, (128 - 4 * i) % 128, 1)
                b = pltpu.roll(after, (132 - 4 * i) % 128, 1)
                edge[i] = jnp.where(lane < 4, a, jnp.where(lane < 8, b, 0.0))
            x = jnp.concatenate([vals[4 * g + i, h] for i in range(4)], axis=0)
            xh, xl = halves(x.reshape(256, W))
            eh, el = halves(edge[...].reshape(256, 128))
            summed = (
                jnp.dot(xh, band, preferred_element_type=F32)
                + jnp.dot(xl, band, preferred_element_type=F32)
                + jnp.dot(eh, eband, preferred_element_type=F32)
                + jnp.dot(el, eband, preferred_element_type=F32)
            )
            detail = x - summed.reshape(32, 8, W) * share
            for i in range(4):
                det[4 * g + i, h] = detail[8 * i : 8 * i + 8]

    def both(s):
        return s + pltpu.roll(s, RB, 0)

    def reduce_all(step):
        sends = []
        for p in range(1, 8):
            peer = lax.rem(ang + p, 8)
            cp = to_ang(part.at[step, peer], got.at[step, p], xs.at[step, p], xr.at[step, p], peer)
            cp.start()
            sends.append(cp)
        for cp in sends:
            cp.wait_recv()
        for t in range(2):
            num = part[step, ang, 0, t]
            den = part[step, ang, 1, t]
            for p in range(1, 8):
                num = num + got[step, p, 0, t]
                den = den + got[step, p, 1, t]
            final[step, ang, t] = num / den
        gathers = []
        for p in range(1, 8):
            peer = lax.rem(ang + p, 8)
            cp = to_ang(final.at[step, ang], final.at[step, ang], ys.at[step, p], yr.at[step, p], peer)
            cp.start()
            gathers.append(cp)
        for p in range(1, 8):
            gathers[p - 1].wait_recv()

        @pl.loop(0, 8)
        def _(m):
            for t in range(2):
                tile = final[step, m, t]
                turned = pltpu.roll(tile, RB, 0)
                gmap[4 * m + 2 * t] = jnp.where(low, tile, turned)
                gmap[4 * m + 2 * t + 1] = jnp.where(low, turned, tile)

        return sends + gathers

    pending = []

    @pl.loop(0, 8)
    def _(m):
        for t in range(2):
            sums = []
            for b in range(2):
                block = 4 * m + 2 * t + b
                sums.append(both(jnp.sum(det[block, 0], axis=0) + jnp.sum(det[block, 1], axis=0)))
            part[0, m, 0, t] = jnp.where(low, sums[0], sums[1])
            part[0, m, 1, t] = jnp.full((8, W), 32.0, F32)

    pending += reduce_all(0)
    for step in range(1, ITERS + 1):
        @pl.loop(0, 8)
        def _(m):
            for t in range(2):
                nums, dens = [], []
                for b in range(2):
                    block = 4 * m + 2 * t + b
                    gain = gmap[block][None]
                    num = jnp.zeros((8, W), F32)
                    den = jnp.zeros((8, W), F32)
                    for h in range(2):
                        d = det[block, h]
                        scaled = (d - gain) / 0.2
                        weight = 1.0 / (1.0 + scaled * scaled)
                        num = num + jnp.sum(weight * d, axis=0)
                        den = den + jnp.sum(weight, axis=0)
                    nums.append(both(num))
                    dens.append(both(den))
                part[step, m, 0, t] = jnp.where(low, nums[0], nums[1])
                part[step, m, 1, t] = jnp.where(low, dens[0], dens[1])

        pending += reduce_all(step)
        if step < ITERS:
            for d in (1, 3, 2)[0 : 2] if step == 1 else (2,):
                for h in range(2):
                    arrived(h, d)
                    second_hop(h, d)

    give = []
    for p in range(NDET):
        owner = lax.rem(me + p, NDET)
        for t in range(2):
            a = gmap[plan[CHOSEN + owner * MOST + 2 * t]]
            b = gmap[plan[CHOSEN + owner * MOST + 2 * t + 1]]
            gslot[p, t] = jnp.where(low, a, b)
        if p == 0:
            cp = pltpu.make_async_copy(gslot.at[p], gains.at[me], gs.at[p])
            stay.append(cp)
        else:
            cp = to_det(gslot.at[p], gains.at[me], gs.at[p], gr.at[p], owner)
            give.append(cp)
        cp.start()

    for cp in give + second:
        cp.wait_recv()
    for cp in stay:
        cp.wait()
    for cp in give + second + halos + pending + [c for _, _, c in first]:
        cp.wait_send()


def move(cap, plan, raw, dark, flat):
    chunk = (8, 8, W)
    dma = pltpu.SemaphoreType.DMA
    scratch = [
        pltpu.VMEM((2, 16, 128, W), F32),
        pltpu.VMEM((NBLK, 2) + chunk, F32),
        pltpu.VMEM((NBLK, 2) + chunk, F32),
        pltpu.VMEM((NBLK, 8, W), F32),
        pltpu.VMEM((3, cap) + chunk, F32),
        pltpu.VMEM((3, cap) + chunk, F32),
    ]
    scratch += [pltpu.VMEM((cap,) + chunk, F32) for _ in range(6)]
    scratch += [
        pltpu.VMEM((4, 4, MOST) + chunk, F32),
        pltpu.VMEM((4, 4, MOST) + chunk, F32),
        pltpu.VMEM((2, 2, 8, 8, 128), F32),
        pltpu.VMEM((2, 2, 8, 8, 128), F32),
        pltpu.VMEM((32, 8, 128), F32),
        pltpu.VMEM((ITERS + 1, 8, 2, 2, 8, W), F32),
        pltpu.VMEM((ITERS + 1, 8, 2, 2, 8, W), F32),
        pltpu.VMEM((ITERS + 1, 8, 2, 8, W), F32),
        pltpu.VMEM((NDET, 2, 8, W), F32),
        dma((2,)),
        dma((2, 4)), dma((2, 4)),
        dma((2, 4, 4)), dma((2, 4, 4)),
        dma((2, 4)),
        dma((2, 2)), dma((2, 2)),
        dma((ITERS + 1, 8)), dma((ITERS + 1, 8)), dma((ITERS + 1, 8)), dma((ITERS + 1, 8)),
        dma((NDET,)), dma((NDET,)),
    ]
    smem = pl.BlockSpec(memory_space=pltpu.SMEM)
    vmem = pl.BlockSpec(memory_space=pltpu.VMEM)
    hbm = pl.BlockSpec(memory_space=pl.ANY)
    return pl.pallas_call(
        functools.partial(move_kernel, cap),
        out_shape=(
            jax.ShapeDtypeStruct((NDET, 2, MOST) + chunk, F32),
            jax.ShapeDtypeStruct((NDET, 2, 8, W), F32),
        ),
        in_specs=[smem, hbm, vmem, vmem],
        out_specs=(hbm, hbm),
        scratch_shapes=scratch,
        compiler_params=pltpu.CompilerParams(
            collective_id=cap, has_side_effects=True, vmem_limit_bytes=56 * 2**20
        ),
        name=f"move{cap}",
    )(plan, raw, dark, flat)


def rebin_kernel(plan, slabs_hbm, gains, offsets, weights, out, slabs, lhs, rhs, low_rhs, sems):
    c = pl.program_id(0)
    me = lax.axis_index("det")

    def load(i):
        return pltpu.make_async_copy(slabs_hbm.at[i], slabs.at[i], sems.at[i])

    @pl.when(c == 0)
    def _():
        @pl.loop(0, NDET)
        def _(i):
            load(i).start()

        rhs[...] = jnp.zeros(rhs.shape, BF16)
        low_rhs[...] = jnp.zeros(low_rhs.shape, BF16)
        load(0).wait()

    @pl.when(c < NDET - 1)
    def _():
        load(c + 1).wait()

    rel = offsets[...] - c * W
    wts = weights[...]

    def coefficients(row, cols):
        ahead = row - rel[:, cols]
        total = jnp.zeros(ahead.shape, F32)
        for k in range(BW):
            total = jnp.where(ahead == k, wts[k : k + 1, cols], total)
        return halves(total)

    for start, cols in ((0, slice(0, 128)), (112, slice(128, 256))):
        high, small = coefficients(start + lax.broadcasted_iota(jnp.int32, (144, 128), 0), cols)
        rhs[start : start + 144, cols] = high
        rhs[W + start : W + start + 144, cols] = high
        low_rhs[start : start + 144, cols] = small
    row = lax.broadcasted_iota(jnp.int32, (16, W), 0)
    high, small = coefficients(jnp.where(row < 8, row - 8, row + (W - 8)), slice(0, W))
    rhs[2 * W : 2 * W + 16, :] = high
    rhs[2 * W + 16 : 2 * W + 32, :] = high
    rhs[2 * W + 32 : 2 * W + 48, :] = small

    low = lax.broadcasted_iota(jnp.int32, (8, W), 0) < RB
    lane = lax.broadcasted_iota(jnp.int32, (1, 1, 128), 2)
    before = jnp.maximum(c - 1, 0)
    after = jnp.minimum(c + 1, NDET - 1)

    def gain(chunk, j):
        tile = gains[chunk, j // 2]
        turned = pltpu.roll(tile, RB, 0)
        return jnp.where(low, tile, turned) if j % 2 == 0 else jnp.where(low, turned, tile)

    for j in range(MOST):
        on = plan[FILLED + me * MOST + j].astype(F32)
        g = (gain(c, j) * on)[None]
        ge = (jnp.where(lane[0] >= 64, gain(before, j)[:, 128:], gain(after, j)[:, :128]) * on)[None]
        for h in range(2):
            rows = slice((h * MOST + j) * 64, (h * MOST + j) * 64 + 64)
            x = slabs[c, h, j] * on - g
            a, b = halves(x.reshape(64, W))
            lhs[rows, 0:W] = a
            lhs[rows, W : 2 * W] = b
            e = jnp.where(lane >= 64, slabs[before, h, j, :, :, 128:], slabs[after, h, j, :, :, :128])
            e = (e * on - ge).reshape(64, 128)
            e = jnp.where(lane[0] < 16, pltpu.roll(e, 8, 1), 0.0)
            e = e + pltpu.roll(e, 16, 1) + pltpu.roll(e, 32, 1)
            a, b = halves(e)
            middle = (lane[0] >= 16) & (lane[0] < 32)
            lhs[rows, 2 * W :] = jnp.where(middle, b.astype(F32), a.astype(F32)).astype(BF16)
    for h in range(2):
        for j in range(MOST):
            rows = slice((h * MOST + j) * 64, (h * MOST + j) * 64 + 64)
            acc = jnp.dot(lhs[rows, :], rhs[...], preferred_element_type=F32)
            acc = acc + jnp.dot(lhs[rows, 0:W], low_rhs[...], preferred_element_type=F32)
            out[16 * h : 16 * h + 16, j] = acc.reshape(16, RB, W)


def rebin(plan, slabs, gains, offsets, weights):
    return pl.pallas_call(
        rebin_kernel,
        grid=(NDET,),
        out_shape=jax.ShapeDtypeStruct((32, MOST, RB, COLS), F32),
        in_specs=[
            pl.BlockSpec(memory_space=pltpu.SMEM),
            pl.BlockSpec(memory_space=pl.ANY),
            pl.BlockSpec((NDET, 2, 8, W), lambda c: (0, 0, 0, 0)),
            pl.BlockSpec((1, W), lambda c: (0, c)),
            pl.BlockSpec((BW, W), lambda c: (0, c)),
        ],
        out_specs=pl.BlockSpec((32, MOST, RB, W), lambda c: (0, 0, 0, c)),
        scratch_shapes=[
            pltpu.VMEM((NDET, 2, MOST, 8, 8, W), F32),
            pltpu.VMEM((512, 2 * W + 128), BF16),
            pltpu.VMEM((2 * W + 128, W), BF16),
            pltpu.VMEM((W, W), BF16),
            pltpu.SemaphoreType.DMA((NDET,)),
        ],
        compiler_params=pltpu.CompilerParams(vmem_limit_bytes=56 * 2**20),
        name="rebin",
    )(plan, slabs, gains, offsets.reshape(1, COLS), weights)


def body(raw_counts, dark_field, flat_field, destinations, band_offsets, band_weights):
    plan, branch = make_plan(destinations)
    slabs, gains = lax.switch(
        branch[0], [functools.partial(move, cap) for cap in CAPS], plan, raw_counts, dark_field, flat_field
    )
    return rebin(plan, slabs, gains, band_offsets, band_weights)


def solution(mesh):
    placed = (P("ang", None, "det"), P(None, "det"), P(None, "det"), P(), P(), P())
    return jax.shard_map(
        body, mesh=mesh, in_specs=placed, out_specs=P("ang", "det", None, None), check_vma=False
    )
```

```python
import functools

import jax
import jax.numpy as jnp
from jax import lax
from jax.experimental import pallas as pl
from jax.experimental.pallas import tpu as pltpu
from jax.sharding import PartitionSpec as P

RB = 4
SMW = 4
ITERS = 3
BW = 4
MOST = 4
NBLK = 32
NDET = 16
SIDE = 4
W = 256
COLS = NDET * W
CAPS = (9, 10, 11, 16)
MESH = pl.DeviceIdType.MESH
F32 = jnp.float32
BF16 = jnp.bfloat16


def halves(x):
    high = x.astype(BF16)
    return high, (x - high.astype(F32)).astype(BF16)


ZLIST, YLIST, PLAN = 64, 128, 192
LIST = 16
EMPTY = NBLK + (LIST << 6) + (LIST << 11)


def plan_kernel(target, plan, branch, count):
    for i in range(PLAN):
        plan[i] = jnp.int32(EMPTY if i < ZLIST else NBLK)

    for k in range(NDET + 2 * SIDE):
        count[k] = 0

    for b in range(NBLK):
        owner = target[b]
        zg = NDET + (owner >> 2)
        yg = NDET + SIDE + (owner & 3)
        place, zp, yp = count[owner], count[zg], count[yg]
        count[owner] = place + 1
        count[zg] = zp + 1
        count[yg] = yp + 1
        plan[owner * MOST + place] = b + (zp << 6) + (yp << 11)
        plan[ZLIST + (zg - NDET) * LIST + zp] = b
        plan[YLIST + (yg - NDET - SIDE) * LIST + yp] = b

    most = count[NDET]
    for k in range(1, 2 * SIDE):
        most = jnp.maximum(most, count[NDET + k])
    branch[0] = sum(((most > cap).astype(jnp.int32) for cap in CAPS[:-1]), jnp.int32(0))


def make_plan(destinations):
    smem = pl.BlockSpec(memory_space=pltpu.SMEM)
    return pl.pallas_call(
        plan_kernel,
        out_shape=(jax.ShapeDtypeStruct((PLAN,), jnp.int32), jax.ShapeDtypeStruct((1,), jnp.int32)),
        in_specs=[smem],
        out_specs=(smem, smem),
        scratch_shapes=[pltpu.SMEM((NDET + 2 * SIDE,), jnp.int32)],
        name="plan",
    )(destinations.reshape(NBLK))


def move_kernel(cap, plan, raw_hbm, dark, flat, slabs, gains, *scr):
    (raw, vals, det, gmap, sa, sb, ra1, ra2, ra3, rb1, rb2, rb3, ta, tb, halo_out, halo_in, edge, part,
     got, final, gslot, ghalf, raw_sem, s1, r1, s2, r2, loc, hs, hr, xs, xr, ys, yr, gs, gr, ps, pr) = scr
    ra, rb = (None, ra1, ra2, ra3), (None, rb1, rb2, rb3)
    me = lax.axis_index("det")
    ang = lax.axis_index("ang")
    z, y = me // SIDE, me % SIDE
    core = ang % 2

    def at(dz, dy):
        return lax.rem(z + dz, SIDE) * SIDE + lax.rem(y + dy, SIDE)

    def to_det(src, dst, send, recv, where):
        return pltpu.make_async_remote_copy(src, dst, send, recv, device_id={"det": where}, device_id_type=MESH)

    def to_ang(src, dst, send, recv, where):
        return pltpu.make_async_remote_copy(src, dst, send, recv, device_id={"ang": where}, device_id_type=MESH)

    loads = [pltpu.make_async_copy(raw_hbm.at[pl.ds(16 * h, 16)], raw.at[h], raw_sem.at[h]) for h in range(2)]
    for cp in loads:
        cp.start()
    bar = pltpu.get_barrier_semaphore()
    for p in range(1, NDET):
        pl.semaphore_signal(bar, inc=1, device_id={"det": lax.rem(me + p, NDET)}, device_id_type=MESH)
    for p in range(1, 8):
        pl.semaphore_signal(bar, inc=1, device_id={"ang": lax.rem(ang + p, 8)}, device_id_type=MESH)

    low = lax.broadcasted_iota(jnp.int32, (8, W), 0) < RB
    lane = lax.broadcasted_iota(jnp.int32, (8, 128), 1)

    def project(h):
        @pl.loop(0, 16)
        def _(q):
            rows = pl.ds(pl.multiple_of(8 * q, 8), 8)
            d = dark[rows, :]
            x = -jnp.log((raw[h, :, rows, :] - d) / (flat[rows, :] - d))
            x = x.reshape(8, 2, 8, W)
            for p in range(8):
                x0, x1 = x[p, 0], x[p, 1]
                vals[2 * q, h, p] = jnp.where(low, x0, pltpu.roll(x1, RB, 0))
                vals[2 * q + 1, h, p] = jnp.where(low, pltpu.roll(x0, RB, 0), x1)

    def pack(h):
        @pl.loop(0, 8)
        def _(g):
            right = jnp.zeros((8, 128), F32)
            left = jnp.zeros((8, 128), F32)
            for i in range(32):
                x = vals[4 * g + i // 8, h, i % 8]
                here = (lane >= 4 * i) & (lane < 4 * i + 4)
                right = jnp.where(here, pltpu.roll(x[:, 128:], (4 * i + 4) % 128, 1), right)
                left = jnp.where(here, pltpu.roll(x[:, :128], 4 * i, 1), left)
            halo_out[h, 0, g] = right
            halo_out[h, 1, g] = left

    halos = []
    first = []
    second = []
    stay = []

    def halo(h):
        for side, where in ((0, lax.rem(me + 1, NDET)), (1, lax.rem(me + NDET - 1, NDET))):
            cp = to_det(halo_out.at[h, side], halo_in.at[h, side], hs.at[h, side], hr.at[h, side], where)
            cp.start()
            halos.append(cp)

    def first_hop(h):
        listing, out, into = (ZLIST, sa, ra) if h == 0 else (YLIST, sb, rb)
        for d in (1, 3, 2):
            group = lax.rem((z if h == 0 else y) + d, SIDE)

            @pl.loop(0, cap)
            def _(c):
                out[d - 1, c] = vals[plan[listing + group * LIST + c], h]

            where = at(d, 0) if h == 0 else at(0, d)
            cp = to_det(out.at[d - 1], into[d].at[pl.ds(0, cap)], s1.at[h, d], r1.at[h, d], where)
            cp.start()
            first.append((h, d, cp))

    def second_hop(h, d):
        out = ta if h == 0 else tb
        col = at(SIDE - d, 0) if h == 0 else at(0, SIDE - d)
        for e in (1, 3, 2, 0):
            owner = at(0, e) if h == 0 else at(e, 0)
            for j in range(MOST):
                word = plan[owner * MOST + j]
                if d == 0:
                    out[d, e, j] = vals[word & 63, h]
                elif h == 0:
                    out[d, e, j] = ra[d][jnp.minimum((word >> 6) & 31, cap)]
                else:
                    out[d, e, j] = rb[d][jnp.minimum(word >> 11, cap)]
            if e == 0:
                cp = pltpu.make_async_copy(out.at[d, e], slabs.at[col, h], loc.at[h, d])
                stay.append(cp)
            else:
                cp = to_det(out.at[d, e], slabs.at[col, h], s2.at[h, d, e], r2.at[h, d, e], owner)
                second.append(cp)
            cp.start()

    def arrived(h, dist):
        for hh, d, cp in first:
            if hh == h and d == dist:
                cp.wait_recv()

    nothing = jnp.zeros((8, 8, W), F32)
    for h in range(2):
        vals[NBLK, h] = nothing
        for d in range(1, SIDE):
            (ra, rb)[h][d][cap] = nothing
    gmap[NBLK] = nothing[0]
    loads[0].wait()
    project(0)
    pack(0)
    loads[1].wait()
    project(1)
    pl.semaphore_wait(bar, NDET - 1 + 7)
    first_hop(0)
    halo(0)
    pack(1)
    halo(1)
    first_hop(1)
    second_hop(0, 0)
    second_hop(1, 0)

    src = lax.broadcasted_iota(jnp.int32, (W, W), 0)
    dst = lax.broadcasted_iota(jnp.int32, (W, W), 1)
    band = (jnp.abs(src - dst) <= SMW).astype(BF16)
    erow = lax.broadcasted_iota(jnp.int32, (128, W), 0)
    ecol = lax.broadcasted_iota(jnp.int32, (128, W), 1)
    at_left = (erow < 4) & (ecol <= erow)
    at_right = (erow >= 4) & (erow < 8) & (W + (erow - 4) - ecol <= SMW)
    eband = (at_left | at_right).astype(BF16)
    col = me * W + lax.broadcasted_iota(jnp.int32, (8, W), 1)
    number = jnp.minimum(col + SMW, COLS - 1) - jnp.maximum(col - SMW, 0) + 1
    share = (1.0 / number.astype(F32))[None]
    for cp in halos:
        cp.wait_recv()
    for h in range(2):
        @pl.loop(0, 8)
        def _(g):
            before = jnp.where(me == 0, 0.0, halo_in[h, 0, g])
            after = jnp.where(me == NDET - 1, 0.0, halo_in[h, 1, g])
            for i in range(32):
                a = pltpu.roll(before, (128 - 4 * i) % 128, 1)
                b = pltpu.roll(after, (132 - 4 * i) % 128, 1)
                edge[i] = jnp.where(lane < 4, a, jnp.where(lane < 8, b, 0.0))
            x = jnp.concatenate([vals[4 * g + i, h] for i in range(4)], axis=0)
            xh, xl = halves(x.reshape(256, W))
            eh, el = halves(edge[...].reshape(256, 128))
            summed = (
                jnp.dot(xh, band, preferred_element_type=F32)
                + jnp.dot(xl, band, preferred_element_type=F32)
                + jnp.dot(eh, eband, preferred_element_type=F32)
                + jnp.dot(el, eband, preferred_element_type=F32)
            )
            detail = x - summed.reshape(32, 8, W) * share
            for i in range(4):
                det[4 * g + i, h] = detail[8 * i : 8 * i + 8]

    def both(s):
        return s + pltpu.roll(s, RB, 0)

    def reduce_all(step):
        sends = []
        for p in range(1, 8):
            peer = lax.rem(ang + p, 8)
            cp = to_ang(part.at[step, peer], got.at[step, p], xs.at[step, p], xr.at[step, p], peer)
            cp.start()
            sends.append(cp)
        for cp in sends:
            cp.wait_recv()
        for t in range(2):
            num = part[step, ang, 0, t]
            den = part[step, ang, 1, t]
            for p in range(1, 8):
                num = num + got[step, p, 0, t]
                den = den + got[step, p, 1, t]
            final[step, ang, t] = num / den
        gathers = []
        for p in range(1, 8):
            peer = lax.rem(ang + p, 8)
            cp = to_ang(final.at[step, ang], final.at[step, ang], ys.at[step, p], yr.at[step, p], peer)
            cp.start()
            gathers.append(cp)
        for p in range(1, 8):
            gathers[p - 1].wait_recv()

        @pl.loop(0, 8)
        def _(m):
            for t in range(2):
                tile = final[step, m, t]
                turned = pltpu.roll(tile, RB, 0)
                gmap[4 * m + 2 * t] = jnp.where(low, tile, turned)
                gmap[4 * m + 2 * t + 1] = jnp.where(low, turned, tile)

        return sends + gathers

    pending = []

    @pl.loop(0, 8)
    def _(m):
        for t in range(2):
            sums = []
            for b in range(2):
                block = 4 * m + 2 * t + b
                sums.append(both(jnp.sum(det[block, 0], axis=0) + jnp.sum(det[block, 1], axis=0)))
            part[0, m, 0, t] = jnp.where(low, sums[0], sums[1])
            part[0, m, 1, t] = jnp.full((8, W), 32.0, F32)

    pending += reduce_all(0)
    for step in range(1, ITERS + 1):
        @pl.loop(0, 8)
        def _(m):
            for t in range(2):
                nums, dens = [], []
                for b in range(2):
                    block = 4 * m + 2 * t + b
                    gain = gmap[block][None]
                    num = jnp.zeros((8, W), F32)
                    den = jnp.zeros((8, W), F32)
                    for h in range(2):
                        d = det[block, h]
                        scaled = (d - gain) * 5.0
                        weight = 1.0 / (1.0 + scaled * scaled)
                        num = num + jnp.sum(weight * d, axis=0)
                        den = den + jnp.sum(weight, axis=0)
                    nums.append(both(num))
                    dens.append(both(den))
                part[step, m, 0, t] = jnp.where(low, nums[0], nums[1])
                part[step, m, 1, t] = jnp.where(low, dens[0], dens[1])

        pending += reduce_all(step)
        if step == 1:
            for d in (1, 3):
                for h in range(2):
                    arrived(h, d)
                    second_hop(h, d)

    give = []
    for p in range(NDET):
        owner = lax.rem(me + p, NDET)
        a = gmap[plan[owner * MOST + 2 * core] & 63]
        b = gmap[plan[owner * MOST + 2 * core + 1] & 63]
        gslot[p] = jnp.where(low, a, b)
        if p == 0:
            cp = pltpu.make_async_copy(gslot.at[p], ghalf.at[me], gs.at[p])
        else:
            cp = to_det(gslot.at[p], ghalf.at[me], gs.at[p], gr.at[p], owner)
            give.append(cp)
        cp.start()
        if p == 0:
            mine = cp
    for h in range(2):
        arrived(h, 2)
        second_hop(h, 2)
    mine.wait()
    for cp in give:
        cp.wait_recv()
    swap = to_ang(ghalf, gains.at[core], ps, pr, ang + 1 - 2 * core)
    swap.start()
    keep = pltpu.make_async_copy(ghalf, gains.at[core], gs.at[0])
    keep.start()
    stay.append(keep)

    swap.wait_recv()
    for cp in second:
        cp.wait_recv()
    for cp in stay:
        cp.wait()
    for cp in [swap] + give + second + halos + pending + [c for _, _, c in first]:
        cp.wait_send()


def move(cap, plan, raw, dark, flat):
    chunk = (8, 8, W)
    dma = pltpu.SemaphoreType.DMA
    scratch = [
        pltpu.VMEM((2, 16, 128, W), F32),
        pltpu.VMEM((NBLK + 1, 2) + chunk, F32),
        pltpu.VMEM((NBLK, 2) + chunk, F32),
        pltpu.VMEM((NBLK + 1, 8, W), F32),
        pltpu.VMEM((3, cap) + chunk, F32),
        pltpu.VMEM((3, cap) + chunk, F32),
    ]
    scratch += [pltpu.VMEM((cap + 1,) + chunk, F32) for _ in range(6)]
    scratch += [
        pltpu.VMEM((4, 4, MOST) + chunk, F32),
        pltpu.VMEM((4, 4, MOST) + chunk, F32),
        pltpu.VMEM((2, 2, 8, 8, 128), F32),
        pltpu.VMEM((2, 2, 8, 8, 128), F32),
        pltpu.VMEM((32, 8, 128), F32),
        pltpu.VMEM((ITERS + 1, 8, 2, 2, 8, W), F32),
        pltpu.VMEM((ITERS + 1, 8, 2, 2, 8, W), F32),
        pltpu.VMEM((ITERS + 1, 8, 2, 8, W), F32),
        pltpu.VMEM((NDET, 8, W), F32),
        pltpu.VMEM((NDET, 8, W), F32),
        dma((2,)),
        dma((2, 4)), dma((2, 4)),
        dma((2, 4, 4)), dma((2, 4, 4)),
        dma((2, 4)),
        dma((2, 2)), dma((2, 2)),
        dma((ITERS + 1, 8)), dma((ITERS + 1, 8)), dma((ITERS + 1, 8)), dma((ITERS + 1, 8)),
        dma((NDET,)), dma((NDET,)), dma(()), dma(()),
    ]
    smem = pl.BlockSpec(memory_space=pltpu.SMEM)
    vmem = pl.BlockSpec(memory_space=pltpu.VMEM)
    hbm = pl.BlockSpec(memory_space=pl.ANY)
    return pl.pallas_call(
        functools.partial(move_kernel, cap),
        out_shape=(
            jax.ShapeDtypeStruct((NDET, 2, MOST) + chunk, F32),
            jax.ShapeDtypeStruct((2, NDET, 8, W), F32),
        ),
        in_specs=[smem, hbm, vmem, vmem],
        out_specs=(hbm, hbm),
        scratch_shapes=scratch,
        compiler_params=pltpu.CompilerParams(
            collective_id=cap, has_side_effects=True, vmem_limit_bytes=56 * 2**20
        ),
        name=f"move{cap}",
    )(plan, raw, dark, flat)


def rebin_kernel(slabs_hbm, gains, offsets, weights, out, slabs, lhs0, lhs1, rhs0, rhs1, low0, low1, sems):
    i = pl.program_id(0)
    pair = ((lhs0, rhs0, low0), (lhs1, rhs1, low1))

    def load(n):
        return pltpu.make_async_copy(slabs_hbm.at[n], slabs.at[n], sems.at[n])

    low = lax.broadcasted_iota(jnp.int32, (8, W), 0) < RB
    lane = lax.broadcasted_iota(jnp.int32, (8, 128), 1)[None]
    second = (lane >= 64) & (lane < 80)
    third = (lane >= 32) & (lane < 48)

    def prepare(c, lhs, rhs, low_rhs):
        here = pl.ds(pl.multiple_of(c * W, W), W)
        rel = offsets[:, here] - c * W
        wts = weights[:, here]

        def coefficients(row, cols):
            ahead = row - rel[:, cols]
            total = jnp.zeros(ahead.shape, F32)
            for k in range(BW):
                total = jnp.where(ahead == k, wts[k : k + 1, cols], total)
            return halves(total)

        for start, cols in ((0, slice(0, 128)), (112, slice(128, 256))):
            high, small = coefficients(start + lax.broadcasted_iota(jnp.int32, (144, 128), 0), cols)
            rhs[start : start + 144, cols] = high
            rhs[W + start : W + start + 144, cols] = high
            low_rhs[start : start + 144, cols] = small
        row = lax.broadcasted_iota(jnp.int32, (16, W), 0)
        high, small = coefficients(jnp.where(row < 8, row - 8, row + (W - 8)), slice(0, W))
        high32 = high.astype(F32)
        none = jnp.zeros((8, W), F32)
        rhs[2 * W : 2 * W + 16, :] = jnp.concatenate([high32[8:], none], axis=0).astype(BF16)
        rhs[2 * W + 32 : 2 * W + 48, :] = small
        rhs[2 * W + 64 : 2 * W + 80, :] = high
        rhs[2 * W + 112 : 2 * W + 128, :] = jnp.concatenate([none, high32[:8]], axis=0).astype(BF16)

        before = jnp.maximum(c - 1, 0)
        after = jnp.minimum(c + 1, NDET - 1)

        def gain(chunk, j):
            tile = gains[j // 2, chunk]
            turned = pltpu.roll(tile, RB, 0)
            return jnp.where(low, tile, turned) if j % 2 == 0 else jnp.where(low, turned, tile)

        for j in range(MOST):
            g = gain(c, j)[None]
            ge = jnp.where(lane >= 64, gain(before, j)[None, :, 128:], gain(after, j)[None, :, :128])
            for h in range(2):
                rows = slice((h * MOST + j) * 64, (h * MOST + j) * 64 + 64)
                a, b = halves((slabs[c, h, j] - g).reshape(64, W))
                lhs[rows, 0:W] = a
                lhs[rows, W : 2 * W] = b
                e = jnp.where(lane >= 64, slabs[before, h, j, :, :, 128:], slabs[after, h, j, :, :, :128]) - ge
                e = jnp.where(second, pltpu.roll(e, 72, 2), jnp.where(third, pltpu.roll(e, 40, 2), e))
                high = e.astype(BF16).astype(F32)
                e = jnp.where(second, e - high, high)
                lhs[rows, 2 * W :] = e.reshape(64, 128).astype(BF16)

    def product(side, lhs, rhs, low_rhs):
        acc = jnp.dot(lhs[...], rhs[...], preferred_element_type=F32)
        acc = acc + jnp.dot(lhs[:, 0:W], low_rhs[...], preferred_element_type=F32)
        for h in range(2):
            for j in range(MOST):
                rows = slice((h * MOST + j) * 64, (h * MOST + j) * 64 + 64)
                out[16 * h : 16 * h + 16, j, :, side * W : side * W + W] = acc[rows].reshape(16, RB, W)

    @pl.when(i == 0)
    def _():
        @pl.loop(0, NDET)
        def _(n):
            load(n).start()

        for _, rhs, low_rhs in pair:
            rhs[...] = jnp.zeros(rhs.shape, BF16)
            low_rhs[...] = jnp.zeros(low_rhs.shape, BF16)
        load(0).wait()
        load(1).wait()
        prepare(0, *pair[0])

    @pl.when(i < NDET // 2 - 1)
    def _():
        load(2 * i + 2).wait()
        load(2 * i + 3).wait()

    prepare(2 * i + 1, *pair[1])
    product(0, *pair[0])
    prepare(jnp.minimum(2 * i + 2, NDET - 1), *pair[0])
    product(1, *pair[1])


def rebin(slabs, gains, offsets, weights):
    return pl.pallas_call(
        rebin_kernel,
        grid=(NDET // 2,),
        out_shape=jax.ShapeDtypeStruct((32, MOST, RB, COLS), F32),
        in_specs=[
            pl.BlockSpec(memory_space=pl.ANY),
            pl.BlockSpec((2, NDET, 8, W), lambda c: (0, 0, 0, 0)),
            pl.BlockSpec((1, COLS), lambda c: (0, 0)),
            pl.BlockSpec((BW, COLS), lambda c: (0, 0)),
        ],
        out_specs=pl.BlockSpec((32, MOST, RB, 2 * W), lambda c: (0, 0, 0, c)),
        scratch_shapes=[pltpu.VMEM((NDET, 2, MOST, 8, 8, W), F32)]
        + [pltpu.VMEM((512, 2 * W + 128), BF16)] * 2
        + [pltpu.VMEM((2 * W + 128, W), BF16)] * 2
        + [pltpu.VMEM((W, W), BF16)] * 2
        + [pltpu.SemaphoreType.DMA((NDET,))],
        compiler_params=pltpu.CompilerParams(vmem_limit_bytes=56 * 2**20),
        name="rebin",
    )(slabs, gains, offsets.reshape(1, COLS), weights)


def body(raw_counts, dark_field, flat_field, destinations, band_offsets, band_weights):
    plan, branch = make_plan(destinations)
    slabs, gains = lax.switch(
        branch[0], [functools.partial(move, cap) for cap in CAPS], plan, raw_counts, dark_field, flat_field
    )
    return rebin(slabs, gains, band_offsets, band_weights)


def solution(mesh):
    placed = (P("ang", None, "det"), P(None, "det"), P(None, "det"), P(), P(), P())
    return jax.shard_map(
        body, mesh=mesh, in_specs=placed, out_specs=P("ang", "det", None, None), check_vma=False
    )
```

```python
import functools

import jax
import jax.numpy as jnp
from jax import lax
from jax.experimental import pallas as pl
from jax.experimental.pallas import tpu as pltpu
from jax.sharding import PartitionSpec as P

RB = 4
SMW = 4
ITERS = 3
BW = 4
MOST = 4
NBLK = 32
NDET = 16
SIDE = 4
W = 256
COLS = NDET * W
CAPS = (9, 10, 11, 16)
MESH = pl.DeviceIdType.MESH
F32 = jnp.float32
BF16 = jnp.bfloat16


def halves(x):
    high = x.astype(BF16)
    return high, (x - high.astype(F32)).astype(BF16)


ZLIST, YLIST, PLAN = 64, 128, 192
LIST = 16
HEAD = 2
EMPTY = NBLK + (LIST << 6) + (LIST << 11)


def plan_kernel(target, plan, branch, count):
    for i in range(PLAN):
        plan[i] = jnp.int32(EMPTY if i < ZLIST else NBLK)

    for k in range(NDET + 2 * SIDE):
        count[k] = 0

    for b in range(NBLK):
        owner = target[b]
        zg = NDET + (owner >> 2)
        yg = NDET + SIDE + (owner & 3)
        place, zp, yp = count[owner], count[zg], count[yg]
        count[owner] = place + 1
        count[zg] = zp + 1
        count[yg] = yp + 1
        plan[owner * MOST + place] = b + (zp << 6) + (yp << 11)
        plan[ZLIST + (zg - NDET) * LIST + zp] = b
        plan[YLIST + (yg - NDET - SIDE) * LIST + yp] = b

    most = count[NDET]
    for k in range(1, 2 * SIDE):
        most = jnp.maximum(most, count[NDET + k])
    branch[0] = sum(((most > cap).astype(jnp.int32) for cap in CAPS[:-1]), jnp.int32(0))


def make_plan(destinations):
    smem = pl.BlockSpec(memory_space=pltpu.SMEM)
    return pl.pallas_call(
        plan_kernel,
        out_shape=(jax.ShapeDtypeStruct((PLAN,), jnp.int32), jax.ShapeDtypeStruct((1,), jnp.int32)),
        in_specs=[smem],
        out_specs=(smem, smem),
        scratch_shapes=[pltpu.SMEM((NDET + 2 * SIDE,), jnp.int32)],
        name="plan",
    )(destinations.reshape(NBLK))


def move_kernel(cap, plan, raw_hbm, dark, flat, slabs, gains, *scr):
    (raw, vals, det, gmap, sa, sb, ra1, ra2, ra3, rb1, rb2, rb3, ta, tb, halo_out, halo_in, edge, part,
     got, final, gslot, ghalf, raw_sem, s1, r1, s2, r2, loc, hs, hr, xs, xr, ys, yr, gs, gr, ps, pr) = scr
    ra, rb = (None, ra1, ra2, ra3), (None, rb1, rb2, rb3)
    me = lax.axis_index("det")
    ang = lax.axis_index("ang")
    z, y = me // SIDE, me % SIDE
    core = ang % 2

    def at(dz, dy):
        return lax.rem(z + dz, SIDE) * SIDE + lax.rem(y + dy, SIDE)

    def to_det(src, dst, send, recv, where):
        return pltpu.make_async_remote_copy(src, dst, send, recv, device_id={"det": where}, device_id_type=MESH)

    def to_ang(src, dst, send, recv, where):
        return pltpu.make_async_remote_copy(src, dst, send, recv, device_id={"ang": where}, device_id_type=MESH)

    loads = [pltpu.make_async_copy(raw_hbm.at[pl.ds(16 * h, 16)], raw.at[h], raw_sem.at[h]) for h in range(2)]
    for cp in loads:
        cp.start()
    bar = pltpu.get_barrier_semaphore()
    for p in range(1, NDET):
        pl.semaphore_signal(bar, inc=1, device_id={"det": lax.rem(me + p, NDET)}, device_id_type=MESH)
    for p in range(1, 8):
        pl.semaphore_signal(bar, inc=1, device_id={"ang": lax.rem(ang + p, 8)}, device_id_type=MESH)

    low = lax.broadcasted_iota(jnp.int32, (8, W), 0) < RB
    lane = lax.broadcasted_iota(jnp.int32, (8, 128), 1)

    def project(h):
        @pl.loop(0, 16)
        def _(q):
            rows = pl.ds(pl.multiple_of(8 * q, 8), 8)
            d = dark[rows, :]
            x = -jnp.log((raw[h, :, rows, :] - d) / (flat[rows, :] - d))
            x = x.reshape(8, 2, 8, W)
            for p in range(8):
                x0, x1 = x[p, 0], x[p, 1]
                vals[2 * q, h, p] = jnp.where(low, x0, pltpu.roll(x1, RB, 0))
                vals[2 * q + 1, h, p] = jnp.where(low, pltpu.roll(x0, RB, 0), x1)

    def pack(h):
        @pl.loop(0, 8)
        def _(g):
            right = jnp.zeros((8, 128), F32)
            left = jnp.zeros((8, 128), F32)
            for i in range(32):
                x = vals[4 * g + i // 8, h, i % 8]
                here = (lane >= 4 * i) & (lane < 4 * i + 4)
                right = jnp.where(here, pltpu.roll(x[:, 128:], (4 * i + 4) % 128, 1), right)
                left = jnp.where(here, pltpu.roll(x[:, :128], 4 * i, 1), left)
            halo_out[h, 0, g] = right
            halo_out[h, 1, g] = left

    halos = []
    first = []
    second = []
    stay = []

    def halo(h):
        for side, where in ((0, lax.rem(me + 1, NDET)), (1, lax.rem(me + NDET - 1, NDET))):
            cp = to_det(halo_out.at[h, side], halo_in.at[h, side], hs.at[h, side], hr.at[h, side], where)
            cp.start()
            halos.append(cp)

    def first_hop(h, dists, start, stop):
        listing, out, into = (ZLIST, sa, ra) if h == 0 else (YLIST, sb, rb)
        for d in dists:
            group = lax.rem((z if h == 0 else y) + d, SIDE)

            @pl.loop(start, stop)
            def _(c):
                out[d - 1, c] = vals[plan[listing + group * LIST + c], h]

            where = at(d, 0) if h == 0 else at(0, d)
            part_of = pl.ds(start, stop - start)
            n = d if start == 0 else 0 if d == 1 else 4
            cp = to_det(out.at[d - 1, part_of], into[d].at[part_of], s1.at[h, n], r1.at[h, n], where)
            cp.start()
            first.append((h, d, cp))

    def second_hop(h, d):
        out = ta if h == 0 else tb
        col = at(SIDE - d, 0) if h == 0 else at(0, SIDE - d)
        for e in (1, 3, 2, 0):
            owner = at(0, e) if h == 0 else at(e, 0)
            for j in range(MOST):
                word = plan[owner * MOST + j]
                if d == 0:
                    out[d, e, j] = vals[word & 63, h]
                elif h == 0:
                    out[d, e, j] = ra[d][jnp.minimum((word >> 6) & 31, cap)]
                else:
                    out[d, e, j] = rb[d][jnp.minimum(word >> 11, cap)]
            if e == 0:
                cp = pltpu.make_async_copy(out.at[d, e], slabs.at[col, h], loc.at[h, d])
                stay.append(cp)
            else:
                cp = to_det(out.at[d, e], slabs.at[col, h], s2.at[h, d, e], r2.at[h, d, e], owner)
                second.append(cp)
            cp.start()

    def arrived(h, dist):
        for hh, d, cp in first:
            if hh == h and d == dist:
                cp.wait_recv()

    nothing = jnp.zeros((8, 8, W), F32)
    for h in range(2):
        vals[NBLK, h] = nothing
        for d in range(1, SIDE):
            (ra, rb)[h][d][cap] = nothing
    gmap[NBLK] = nothing[0]
    loads[0].wait()
    project(0)
    pack(0)
    loads[1].wait()
    project(1)
    pl.semaphore_wait(bar, NDET - 1 + 7)
    first_hop(1, (1, 3), 0, HEAD)
    first_hop(0, (1, 3, 2), 0, cap)
    halo(0)
    pack(1)
    halo(1)
    first_hop(1, (1, 3), HEAD, cap)
    first_hop(1, (2,), 0, cap)
    second_hop(0, 0)
    second_hop(1, 0)

    src = lax.broadcasted_iota(jnp.int32, (W, W), 0)
    dst = lax.broadcasted_iota(jnp.int32, (W, W), 1)
    band = (jnp.abs(src - dst) <= SMW).astype(BF16)
    erow = lax.broadcasted_iota(jnp.int32, (128, W), 0)
    ecol = lax.broadcasted_iota(jnp.int32, (128, W), 1)
    at_left = (erow < 4) & (ecol <= erow)
    at_right = (erow >= 4) & (erow < 8) & (W + (erow - 4) - ecol <= SMW)
    eband = (at_left | at_right).astype(BF16)
    col = me * W + lax.broadcasted_iota(jnp.int32, (8, W), 1)
    number = jnp.minimum(col + SMW, COLS - 1) - jnp.maximum(col - SMW, 0) + 1
    share = (1.0 / number.astype(F32))[None]
    for cp in halos:
        cp.wait_recv()
    for h in range(2):
        @pl.loop(0, 8)
        def _(g):
            before = jnp.where(me == 0, 0.0, halo_in[h, 0, g])
            after = jnp.where(me == NDET - 1, 0.0, halo_in[h, 1, g])
            for i in range(32):
                a = pltpu.roll(before, (128 - 4 * i) % 128, 1)
                b = pltpu.roll(after, (132 - 4 * i) % 128, 1)
                edge[i] = jnp.where(lane < 4, a, jnp.where(lane < 8, b, 0.0))
            x = jnp.concatenate([vals[4 * g + i, h] for i in range(4)], axis=0)
            xh, xl = halves(x.reshape(256, W))
            eh, el = halves(edge[...].reshape(256, 128))
            summed = (
                jnp.dot(xh, band, preferred_element_type=F32)
                + jnp.dot(xl, band, preferred_element_type=F32)
                + jnp.dot(eh, eband, preferred_element_type=F32)
                + jnp.dot(el, eband, preferred_element_type=F32)
            )
            detail = x - summed.reshape(32, 8, W) * share
            for i in range(4):
                det[4 * g + i, h] = detail[8 * i : 8 * i + 8]

    def both(s):
        return s + pltpu.roll(s, RB, 0)

    def reduce_all(step):
        sends = []
        for p in range(1, 8):
            peer = lax.rem(ang + p, 8)
            cp = to_ang(part.at[step, peer], got.at[step, p], xs.at[step, p], xr.at[step, p], peer)
            cp.start()
            sends.append(cp)
        for cp in sends:
            cp.wait_recv()
        for t in range(2):
            num = part[step, ang, 0, t]
            den = part[step, ang, 1, t]
            for p in range(1, 8):
                num = num + got[step, p, 0, t]
                den = den + got[step, p, 1, t]
            final[step, ang, t] = num / den
        gathers = []
        for p in range(1, 8):
            peer = lax.rem(ang + p, 8)
            cp = to_ang(final.at[step, ang], final.at[step, ang], ys.at[step, p], yr.at[step, p], peer)
            cp.start()
            gathers.append(cp)
        for p in range(1, 8):
            gathers[p - 1].wait_recv()

        @pl.loop(0, 8)
        def _(m):
            for t in range(2):
                tile = final[step, m, t]
                turned = pltpu.roll(tile, RB, 0)
                gmap[4 * m + 2 * t] = jnp.where(low, tile, turned)
                gmap[4 * m + 2 * t + 1] = jnp.where(low, turned, tile)

        return sends + gathers

    pending = []

    @pl.loop(0, 8)
    def _(m):
        for t in range(2):
            sums = []
            for b in range(2):
                block = 4 * m + 2 * t + b
                sums.append(both(jnp.sum(det[block, 0], axis=0) + jnp.sum(det[block, 1], axis=0)))
            part[0, m, 0, t] = jnp.where(low, sums[0], sums[1])
            part[0, m, 1, t] = jnp.full((8, W), 32.0, F32)

    pending += reduce_all(0)
    for step in range(1, ITERS + 1):
        @pl.loop(0, 8)
        def _(m):
            for t in range(2):
                nums, dens = [], []
                for b in range(2):
                    block = 4 * m + 2 * t + b
                    gain = gmap[block][None]
                    num = jnp.zeros((8, W), F32)
                    den = jnp.zeros((8, W), F32)
                    for h in range(2):
                        d = det[block, h]
                        scaled = (d - gain) * 5.0
                        weight = 1.0 / (1.0 + scaled * scaled)
                        num = num + jnp.sum(weight * d, axis=0)
                        den = den + jnp.sum(weight, axis=0)
                    nums.append(both(num))
                    dens.append(both(den))
                part[step, m, 0, t] = jnp.where(low, nums[0], nums[1])
                part[step, m, 1, t] = jnp.where(low, dens[0], dens[1])

        pending += reduce_all(step)
        if step == 1:
            for d in (1, 3):
                for h in range(2):
                    arrived(h, d)
                    second_hop(h, d)

    give = []
    for p in range(NDET):
        owner = lax.rem(me + p, NDET)
        a = gmap[plan[owner * MOST + 2 * core] & 63]
        b = gmap[plan[owner * MOST + 2 * core + 1] & 63]
        gslot[p] = jnp.where(low, a, b)
        if p == 0:
            cp = pltpu.make_async_copy(gslot.at[p], ghalf.at[me], gs.at[p])
        else:
            cp = to_det(gslot.at[p], ghalf.at[me], gs.at[p], gr.at[p], owner)
            give.append(cp)
        cp.start()
        if p == 0:
            mine = cp
    for h in range(2):
        arrived(h, 2)
        second_hop(h, 2)
    mine.wait()
    for cp in give:
        cp.wait_recv()
    swap = to_ang(ghalf, gains.at[core], ps, pr, ang + 1 - 2 * core)
    swap.start()
    keep = pltpu.make_async_copy(ghalf, gains.at[core], gs.at[0])
    keep.start()
    stay.append(keep)

    swap.wait_recv()
    for cp in second:
        cp.wait_recv()
    for cp in stay:
        cp.wait()
    for cp in [swap] + give + second + halos + pending + [c for _, _, c in first]:
        cp.wait_send()


def move(cap, plan, raw, dark, flat):
    chunk = (8, 8, W)
    dma = pltpu.SemaphoreType.DMA
    scratch = [
        pltpu.VMEM((2, 16, 128, W), F32),
        pltpu.VMEM((NBLK + 1, 2) + chunk, F32),
        pltpu.VMEM((NBLK, 2) + chunk, F32),
        pltpu.VMEM((NBLK + 1, 8, W), F32),
        pltpu.VMEM((3, cap) + chunk, F32),
        pltpu.VMEM((3, cap) + chunk, F32),
    ]
    scratch += [pltpu.VMEM((cap + 1,) + chunk, F32) for _ in range(6)]
    scratch += [
        pltpu.VMEM((4, 4, MOST) + chunk, F32),
        pltpu.VMEM((4, 4, MOST) + chunk, F32),
        pltpu.VMEM((2, 2, 8, 8, 128), F32),
        pltpu.VMEM((2, 2, 8, 8, 128), F32),
        pltpu.VMEM((32, 8, 128), F32),
        pltpu.VMEM((ITERS + 1, 8, 2, 2, 8, W), F32),
        pltpu.VMEM((ITERS + 1, 8, 2, 2, 8, W), F32),
        pltpu.VMEM((ITERS + 1, 8, 2, 8, W), F32),
        pltpu.VMEM((NDET, 8, W), F32),
        pltpu.VMEM((NDET, 8, W), F32),
        dma((2,)),
        dma((2, 5)), dma((2, 5)),
        dma((2, 4, 4)), dma((2, 4, 4)),
        dma((2, 4)),
        dma((2, 2)), dma((2, 2)),
        dma((ITERS + 1, 8)), dma((ITERS + 1, 8)), dma((ITERS + 1, 8)), dma((ITERS + 1, 8)),
        dma((NDET,)), dma((NDET,)), dma(()), dma(()),
    ]
    smem = pl.BlockSpec(memory_space=pltpu.SMEM)
    vmem = pl.BlockSpec(memory_space=pltpu.VMEM)
    hbm = pl.BlockSpec(memory_space=pl.ANY)
    return pl.pallas_call(
        functools.partial(move_kernel, cap),
        out_shape=(
            jax.ShapeDtypeStruct((NDET, 2, MOST) + chunk, F32),
            jax.ShapeDtypeStruct((2, NDET, 8, W), F32),
        ),
        in_specs=[smem, hbm, vmem, vmem],
        out_specs=(hbm, hbm),
        scratch_shapes=scratch,
        compiler_params=pltpu.CompilerParams(
            collective_id=cap, has_side_effects=True, vmem_limit_bytes=56 * 2**20
        ),
        name=f"move{cap}",
    )(plan, raw, dark, flat)


def rebin_kernel(slabs_hbm, gains, offsets, weights, out, slabs, lhs0, lhs1, rhs0, rhs1, low0, low1, sems):
    i = pl.program_id(0)
    pair = ((lhs0, rhs0, low0), (lhs1, rhs1, low1))

    def load(n):
        return pltpu.make_async_copy(slabs_hbm.at[n], slabs.at[n], sems.at[n])

    low = lax.broadcasted_iota(jnp.int32, (8, W), 0) < RB
    lane = lax.broadcasted_iota(jnp.int32, (8, 128), 1)[None]
    second = (lane >= 64) & (lane < 80)
    third = (lane >= 32) & (lane < 48)

    def prepare(c, lhs, rhs, low_rhs):
        here = pl.ds(pl.multiple_of(c * W, W), W)
        rel = offsets[:, here] - c * W
        wts = weights[:, here]

        def coefficients(row, cols):
            ahead = row - rel[:, cols]
            total = jnp.zeros(ahead.shape, F32)
            for k in range(BW):
                total = jnp.where(ahead == k, wts[k : k + 1, cols], total)
            return halves(total)

        for start, cols in ((0, slice(0, 128)), (112, slice(128, 256))):
            high, small = coefficients(start + lax.broadcasted_iota(jnp.int32, (144, 128), 0), cols)
            rhs[start : start + 144, cols] = high
            rhs[W + start : W + start + 144, cols] = high
            low_rhs[start : start + 144, cols] = small
        row = lax.broadcasted_iota(jnp.int32, (16, W), 0)
        high, small = coefficients(jnp.where(row < 8, row - 8, row + (W - 8)), slice(0, W))
        high32 = high.astype(F32)
        none = jnp.zeros((8, W), F32)
        rhs[2 * W : 2 * W + 16, :] = jnp.concatenate([high32[8:], none], axis=0).astype(BF16)
        rhs[2 * W + 32 : 2 * W + 48, :] = small
        rhs[2 * W + 64 : 2 * W + 80, :] = high
        rhs[2 * W + 112 : 2 * W + 128, :] = jnp.concatenate([none, high32[:8]], axis=0).astype(BF16)

        before = jnp.maximum(c - 1, 0)
        after = jnp.minimum(c + 1, NDET - 1)

        def gain(chunk, j):
            tile = gains[j // 2, chunk]
            turned = pltpu.roll(tile, RB, 0)
            return jnp.where(low, tile, turned) if j % 2 == 0 else jnp.where(low, turned, tile)

        for j in range(MOST):
            g = gain(c, j)[None]
            ge = jnp.where(lane >= 64, gain(before, j)[None, :, 128:], gain(after, j)[None, :, :128])
            for h in range(2):
                rows = slice((h * MOST + j) * 64, (h * MOST + j) * 64 + 64)
                a, b = halves((slabs[c, h, j] - g).reshape(64, W))
                lhs[rows, 0:W] = a
                lhs[rows, W : 2 * W] = b
                e = jnp.where(lane >= 64, slabs[before, h, j, :, :, 128:], slabs[after, h, j, :, :, :128]) - ge
                e = jnp.where(second, pltpu.roll(e, 72, 2), jnp.where(third, pltpu.roll(e, 40, 2), e))
                high = e.astype(BF16).astype(F32)
                lhs[rows, 2 * W :] = jnp.where(second, e - high, e).reshape(64, 128).astype(BF16)

    def product(side, lhs, rhs, low_rhs):
        acc = jnp.dot(lhs[...], rhs[...], preferred_element_type=F32)
        acc = acc + jnp.dot(lhs[:, 0:W], low_rhs[...], preferred_element_type=F32)
        for h in range(2):
            for j in range(MOST):
                rows = slice((h * MOST + j) * 64, (h * MOST + j) * 64 + 64)
                out[16 * h : 16 * h + 16, j, :, side * W : side * W + W] = acc[rows].reshape(16, RB, W)

    @pl.when(i == 0)
    def _():
        for n in range(8):
            load(n).start()

        for _, rhs, low_rhs in pair:
            rhs[...] = jnp.zeros(rhs.shape, BF16)
            low_rhs[...] = jnp.zeros(low_rhs.shape, BF16)
        load(0).wait()
        load(1).wait()
        prepare(0, *pair[0])

    @pl.when(i < NDET // 2 - 4)
    def _():
        load(2 * i + 8).start()
        load(2 * i + 9).start()

    @pl.when(i < NDET // 2 - 1)
    def _():
        load(2 * i + 2).wait()
        load(2 * i + 3).wait()

    prepare(2 * i + 1, *pair[1])
    product(0, *pair[0])
    prepare(jnp.minimum(2 * i + 2, NDET - 1), *pair[0])
    product(1, *pair[1])


def rebin(slabs, gains, offsets, weights):
    return pl.pallas_call(
        rebin_kernel,
        grid=(NDET // 2,),
        out_shape=jax.ShapeDtypeStruct((32, MOST, RB, COLS), F32),
        in_specs=[
            pl.BlockSpec(memory_space=pl.ANY),
            pl.BlockSpec((2, NDET, 8, W), lambda c: (0, 0, 0, 0)),
            pl.BlockSpec((1, COLS), lambda c: (0, 0)),
            pl.BlockSpec((BW, COLS), lambda c: (0, 0)),
        ],
        out_specs=pl.BlockSpec((32, MOST, RB, 2 * W), lambda c: (0, 0, 0, c)),
        scratch_shapes=[pltpu.VMEM((NDET, 2, MOST, 8, 8, W), F32)]
        + [pltpu.VMEM((512, 2 * W + 128), BF16)] * 2
        + [pltpu.VMEM((2 * W + 128, W), BF16)] * 2
        + [pltpu.VMEM((W, W), BF16)] * 2
        + [pltpu.SemaphoreType.DMA((NDET,))],
        compiler_params=pltpu.CompilerParams(vmem_limit_bytes=56 * 2**20),
        name="rebin",
    )(slabs, gains, offsets.reshape(1, COLS), weights)


def body(raw_counts, dark_field, flat_field, destinations, band_offsets, band_weights):
    plan, branch = make_plan(destinations)
    slabs, gains = lax.switch(
        branch[0], [functools.partial(move, cap) for cap in CAPS], plan, raw_counts, dark_field, flat_field
    )
    return rebin(slabs, gains, band_offsets, band_weights)


def solution(mesh):
    placed = (P("ang", None, "det"), P(None, "det"), P(None, "det"), P(), P(), P())
    return jax.shard_map(
        body, mesh=mesh, in_specs=placed, out_specs=P("ang", "det", None, None), check_vma=False
    )
```

```python
import functools

import jax
import jax.numpy as jnp
from jax import lax
from jax.experimental import pallas as pl
from jax.experimental.pallas import tpu as pltpu
from jax.sharding import PartitionSpec as P

RB = 4
SMW = 4
ITERS = 3
BW = 4
MOST = 4
NBLK = 32
NDET = 16
SIDE = 4
W = 256
COLS = NDET * W
CAPS = (9, 10, 11, 16)
MESH = pl.DeviceIdType.MESH
F32 = jnp.float32
BF16 = jnp.bfloat16


def halves(x):
    high = x.astype(BF16)
    return high, (x - high.astype(F32)).astype(BF16)


ZLIST, YLIST, PLAN = 64, 128, 192
LIST = 16
HEAD = 2
EMPTY = NBLK + (LIST << 6) + (LIST << 11)


def plan_kernel(target, plan, branch, count):
    for i in range(PLAN):
        plan[i] = jnp.int32(EMPTY if i < ZLIST else NBLK)

    for k in range(NDET + 2 * SIDE):
        count[k] = 0

    for b in range(NBLK):
        owner = target[b]
        zg = NDET + (owner >> 2)
        yg = NDET + SIDE + (owner & 3)
        place, zp, yp = count[owner], count[zg], count[yg]
        count[owner] = place + 1
        count[zg] = zp + 1
        count[yg] = yp + 1
        plan[owner * MOST + place] = b + (zp << 6) + (yp << 11)
        plan[ZLIST + (zg - NDET) * LIST + zp] = b
        plan[YLIST + (yg - NDET - SIDE) * LIST + yp] = b

    most = count[NDET]
    for k in range(1, 2 * SIDE):
        most = jnp.maximum(most, count[NDET + k])
    branch[0] = sum(((most > cap).astype(jnp.int32) for cap in CAPS[:-1]), jnp.int32(0))


def make_plan(destinations):
    smem = pl.BlockSpec(memory_space=pltpu.SMEM)
    return pl.pallas_call(
        plan_kernel,
        out_shape=(jax.ShapeDtypeStruct((PLAN,), jnp.int32), jax.ShapeDtypeStruct((1,), jnp.int32)),
        in_specs=[smem],
        out_specs=(smem, smem),
        scratch_shapes=[pltpu.SMEM((NDET + 2 * SIDE,), jnp.int32)],
        name="plan",
    )(destinations.reshape(NBLK))


def move_kernel(cap, plan, raw_hbm, dark, flat, slabs, gains, *scr):
    (raw, vals, det, gmap, sa, sb, ra1, ra2, ra3, rb1, rb2, rb3, ta, tb, halo_out, halo_in, edge, part,
     got, final, gslot, ghalf, raw_sem, s1, r1, s2, r2, loc, hs, hr, xs, xr, ys, yr, gs, gr, ps, pr) = scr
    ra, rb = (None, ra1, ra2, ra3), (None, rb1, rb2, rb3)
    me = lax.axis_index("det")
    ang = lax.axis_index("ang")
    z, y = me // SIDE, me % SIDE
    core = ang % 2

    def at(dz, dy):
        return lax.rem(z + dz, SIDE) * SIDE + lax.rem(y + dy, SIDE)

    def to_det(src, dst, send, recv, where):
        return pltpu.make_async_remote_copy(src, dst, send, recv, device_id={"det": where}, device_id_type=MESH)

    def to_ang(src, dst, send, recv, where):
        return pltpu.make_async_remote_copy(src, dst, send, recv, device_id={"ang": where}, device_id_type=MESH)

    loads = [pltpu.make_async_copy(raw_hbm.at[pl.ds(16 * h, 16)], raw.at[h], raw_sem.at[h]) for h in range(2)]
    for cp in loads:
        cp.start()
    bar = pltpu.get_barrier_semaphore()
    for p in range(1, NDET):
        pl.semaphore_signal(bar, inc=1, device_id={"det": lax.rem(me + p, NDET)}, device_id_type=MESH)
    for p in range(1, 8):
        pl.semaphore_signal(bar, inc=1, device_id={"ang": lax.rem(ang + p, 8)}, device_id_type=MESH)

    low = lax.broadcasted_iota(jnp.int32, (8, W), 0) < RB
    lane = lax.broadcasted_iota(jnp.int32, (8, 128), 1)

    def project(h):
        @pl.loop(0, 16)
        def _(q):
            rows = pl.ds(pl.multiple_of(8 * q, 8), 8)
            d = dark[rows, :]
            x = -jnp.log((raw[h, :, rows, :] - d) / (flat[rows, :] - d))
            x = x.reshape(8, 2, 8, W)
            for p in range(8):
                x0, x1 = x[p, 0], x[p, 1]
                vals[2 * q, h, p] = jnp.where(low, x0, pltpu.roll(x1, RB, 0))
                vals[2 * q + 1, h, p] = jnp.where(low, pltpu.roll(x0, RB, 0), x1)

    def pack(h):
        @pl.loop(0, 8)
        def _(g):
            right = jnp.zeros((8, 128), F32)
            left = jnp.zeros((8, 128), F32)
            for i in range(32):
                x = vals[4 * g + i // 8, h, i % 8]
                here = (lane >= 4 * i) & (lane < 4 * i + 4)
                right = jnp.where(here, pltpu.roll(x[:, 128:], (4 * i + 4) % 128, 1), right)
                left = jnp.where(here, pltpu.roll(x[:, :128], 4 * i, 1), left)
            halo_out[h, 0, g] = right
            halo_out[h, 1, g] = left

    halos = []
    first = []
    second = []
    stay = []

    def halo(h):
        for side, where in ((0, lax.rem(me + 1, NDET)), (1, lax.rem(me + NDET - 1, NDET))):
            cp = to_det(halo_out.at[h, side], halo_in.at[h, side], hs.at[h, side], hr.at[h, side], where)
            cp.start()
            halos.append(cp)

    def first_hop(h, dists, start, stop):
        listing, out, into = (ZLIST, sa, ra) if h == 0 else (YLIST, sb, rb)
        for d in dists:
            group = lax.rem((z if h == 0 else y) + d, SIDE)

            @pl.loop(start, stop)
            def _(c):
                out[d - 1, c] = vals[plan[listing + group * LIST + c], h]

            where = at(d, 0) if h == 0 else at(0, d)
            part_of = pl.ds(start, stop - start)
            n = d if start == 0 else 0 if d == 1 else 4
            cp = to_det(out.at[d - 1, part_of], into[d].at[part_of], s1.at[h, n], r1.at[h, n], where)
            cp.start()
            first.append((h, d, cp))

    def second_hop(h, d):
        out = ta if h == 0 else tb
        col = at(SIDE - d, 0) if h == 0 else at(0, SIDE - d)
        for e in (1, 3, 2, 0):
            owner = at(0, e) if h == 0 else at(e, 0)
            for j in range(MOST):
                word = plan[owner * MOST + j]
                if d == 0:
                    out[d, e, j] = vals[word & 63, h]
                elif h == 0:
                    out[d, e, j] = ra[d][jnp.minimum((word >> 6) & 31, cap)]
                else:
                    out[d, e, j] = rb[d][jnp.minimum(word >> 11, cap)]
            if e == 0:
                cp = pltpu.make_async_copy(out.at[d, e], slabs.at[col, h], loc.at[h, d])
                stay.append(cp)
            else:
                cp = to_det(out.at[d, e], slabs.at[col, h], s2.at[h, d, e], r2.at[h, d, e], owner)
                second.append(cp)
            cp.start()

    def arrived(h, dist):
        for hh, d, cp in first:
            if hh == h and d == dist:
                cp.wait_recv()

    nothing = jnp.zeros((8, 8, W), F32)
    for h in range(2):
        vals[NBLK, h] = nothing
        for d in range(1, SIDE):
            (ra, rb)[h][d][cap] = nothing
    gmap[NBLK] = nothing[0]
    loads[0].wait()
    project(0)
    pack(0)
    loads[1].wait()
    project(1)
    pl.semaphore_wait(bar, NDET - 1 + 7)
    first_hop(1, (1, 3), 0, HEAD)
    first_hop(0, (1, 3, 2), 0, cap)
    halo(0)
    pack(1)
    halo(1)
    first_hop(1, (1, 3), HEAD, cap)
    first_hop(1, (2,), 0, cap)
    second_hop(0, 0)
    second_hop(1, 0)

    src = lax.broadcasted_iota(jnp.int32, (W, W), 0)
    dst = lax.broadcasted_iota(jnp.int32, (W, W), 1)
    band = (jnp.abs(src - dst) <= SMW).astype(BF16)
    erow = lax.broadcasted_iota(jnp.int32, (128, W), 0)
    ecol = lax.broadcasted_iota(jnp.int32, (128, W), 1)
    at_left = (erow < 4) & (ecol <= erow)
    at_right = (erow >= 4) & (erow < 8) & (W + (erow - 4) - ecol <= SMW)
    eband = (at_left | at_right).astype(BF16)
    col = me * W + lax.broadcasted_iota(jnp.int32, (8, W), 1)
    number = jnp.minimum(col + SMW, COLS - 1) - jnp.maximum(col - SMW, 0) + 1
    share = (1.0 / number.astype(F32))[None]
    for cp in halos:
        cp.wait_recv()
    for h in range(2):
        @pl.loop(0, 8)
        def _(g):
            before = jnp.where(me == 0, 0.0, halo_in[h, 0, g])
            after = jnp.where(me == NDET - 1, 0.0, halo_in[h, 1, g])
            for i in range(32):
                a = pltpu.roll(before, (128 - 4 * i) % 128, 1)
                b = pltpu.roll(after, (132 - 4 * i) % 128, 1)
                edge[i] = jnp.where(lane < 4, a, jnp.where(lane < 8, b, 0.0))
            x = jnp.concatenate([vals[4 * g + i, h] for i in range(4)], axis=0)
            xh, xl = halves(x.reshape(256, W))
            eh, el = halves(edge[...].reshape(256, 128))
            summed = (
                jnp.dot(xh, band, preferred_element_type=F32)
                + jnp.dot(xl, band, preferred_element_type=F32)
                + jnp.dot(eh, eband, preferred_element_type=F32)
                + jnp.dot(el, eband, preferred_element_type=F32)
            )
            detail = x - summed.reshape(32, 8, W) * share
            for i in range(4):
                det[4 * g + i, h] = detail[8 * i : 8 * i + 8]

    def both(s):
        return s + pltpu.roll(s, RB, 0)

    def reduce_all(step):
        sends = []
        for p in range(1, 8):
            peer = lax.rem(ang + p, 8)
            cp = to_ang(part.at[step, peer], got.at[step, p], xs.at[step, p], xr.at[step, p], peer)
            cp.start()
            sends.append(cp)
        for cp in sends:
            cp.wait_recv()
        for t in range(2):
            num = part[step, ang, 0, t]
            den = part[step, ang, 1, t]
            for p in range(1, 8):
                num = num + got[step, p, 0, t]
                den = den + got[step, p, 1, t]
            final[step, ang, t] = num / den
        gathers = []
        for p in range(1, 8):
            peer = lax.rem(ang + p, 8)
            cp = to_ang(final.at[step, ang], final.at[step, ang], ys.at[step, p], yr.at[step, p], peer)
            cp.start()
            gathers.append(cp)
        for p in range(1, 8):
            gathers[p - 1].wait_recv()

        @pl.loop(0, 8)
        def _(m):
            for t in range(2):
                tile = final[step, m, t]
                turned = pltpu.roll(tile, RB, 0)
                gmap[4 * m + 2 * t] = jnp.where(low, tile, turned)
                gmap[4 * m + 2 * t + 1] = jnp.where(low, turned, tile)

        return sends + gathers

    pending = []

    @pl.loop(0, 8)
    def _(m):
        for t in range(2):
            sums = []
            for b in range(2):
                block = 4 * m + 2 * t + b
                sums.append(both(jnp.sum(det[block, 0], axis=0) + jnp.sum(det[block, 1], axis=0)))
            part[0, m, 0, t] = jnp.where(low, sums[0], sums[1])
            part[0, m, 1, t] = jnp.full((8, W), 32.0, F32)

    pending += reduce_all(0)
    for step in range(1, ITERS + 1):
        @pl.loop(0, 8)
        def _(m):
            for t in range(2):
                nums, dens = [], []
                for b in range(2):
                    block = 4 * m + 2 * t + b
                    gain = gmap[block][None]
                    num = jnp.zeros((8, W), F32)
                    den = jnp.zeros((8, W), F32)
                    for h in range(2):
                        d = det[block, h]
                        scaled = (d - gain) * 5.0
                        weight = 1.0 / (1.0 + scaled * scaled)
                        num = num + jnp.sum(weight * d, axis=0)
                        den = den + jnp.sum(weight, axis=0)
                    nums.append(both(num))
                    dens.append(both(den))
                part[step, m, 0, t] = jnp.where(low, nums[0], nums[1])
                part[step, m, 1, t] = jnp.where(low, dens[0], dens[1])

        pending += reduce_all(step)
        if step == 1:
            for d in (1, 3):
                for h in range(2):
                    arrived(h, d)
                    second_hop(h, d)

    give = []
    for p in range(NDET):
        owner = lax.rem(me + p, NDET)
        a = gmap[plan[owner * MOST + 2 * core] & 63]
        b = gmap[plan[owner * MOST + 2 * core + 1] & 63]
        gslot[p] = jnp.where(low, a, b)
        if p == 0:
            cp = pltpu.make_async_copy(gslot.at[p], ghalf.at[me], gs.at[p])
        else:
            cp = to_det(gslot.at[p], ghalf.at[me], gs.at[p], gr.at[p], owner)
            give.append(cp)
        cp.start()
        if p == 0:
            mine = cp
    for h in range(2):
        arrived(h, 2)
        second_hop(h, 2)
    mine.wait()
    for cp in give:
        cp.wait_recv()
    swap = to_ang(ghalf, gains.at[core], ps, pr, ang + 1 - 2 * core)
    swap.start()
    keep = pltpu.make_async_copy(ghalf, gains.at[core], gs.at[0])
    keep.start()
    stay.append(keep)

    swap.wait_recv()
    for cp in second:
        cp.wait_recv()
    for cp in stay:
        cp.wait()
    for cp in [swap] + give + second + halos + pending + [c for _, _, c in first]:
        cp.wait_send()


def move(cap, plan, raw, dark, flat):
    chunk = (8, 8, W)
    dma = pltpu.SemaphoreType.DMA
    scratch = [
        pltpu.VMEM((2, 16, 128, W), F32),
        pltpu.VMEM((NBLK + 1, 2) + chunk, F32),
        pltpu.VMEM((NBLK, 2) + chunk, F32),
        pltpu.VMEM((NBLK + 1, 8, W), F32),
        pltpu.VMEM((3, cap) + chunk, F32),
        pltpu.VMEM((3, cap) + chunk, F32),
    ]
    scratch += [pltpu.VMEM((cap + 1,) + chunk, F32) for _ in range(6)]
    scratch += [
        pltpu.VMEM((4, 4, MOST) + chunk, F32),
        pltpu.VMEM((4, 4, MOST) + chunk, F32),
        pltpu.VMEM((2, 2, 8, 8, 128), F32),
        pltpu.VMEM((2, 2, 8, 8, 128), F32),
        pltpu.VMEM((32, 8, 128), F32),
        pltpu.VMEM((ITERS + 1, 8, 2, 2, 8, W), F32),
        pltpu.VMEM((ITERS + 1, 8, 2, 2, 8, W), F32),
        pltpu.VMEM((ITERS + 1, 8, 2, 8, W), F32),
        pltpu.VMEM((NDET, 8, W), F32),
        pltpu.VMEM((NDET, 8, W), F32),
        dma((2,)),
        dma((2, 5)), dma((2, 5)),
        dma((2, 4, 4)), dma((2, 4, 4)),
        dma((2, 4)),
        dma((2, 2)), dma((2, 2)),
        dma((ITERS + 1, 8)), dma((ITERS + 1, 8)), dma((ITERS + 1, 8)), dma((ITERS + 1, 8)),
        dma((NDET,)), dma((NDET,)), dma(()), dma(()),
    ]
    smem = pl.BlockSpec(memory_space=pltpu.SMEM)
    vmem = pl.BlockSpec(memory_space=pltpu.VMEM)
    hbm = pl.BlockSpec(memory_space=pl.ANY)
    return pl.pallas_call(
        functools.partial(move_kernel, cap),
        out_shape=(
            jax.ShapeDtypeStruct((NDET, 2, MOST) + chunk, F32),
            jax.ShapeDtypeStruct((2, NDET, 8, W), F32),
        ),
        in_specs=[smem, pl.BlockSpec(memory_space=pltpu.HBM), vmem, vmem],
        out_specs=(hbm, hbm),
        scratch_shapes=scratch,
        compiler_params=pltpu.CompilerParams(
            collective_id=cap, has_side_effects=True, vmem_limit_bytes=(28 + cap) * 2**20
        ),
        name=f"move{cap}",
    )(plan, raw, dark, flat)


def rebin_kernel(slabs_hbm, gains, offsets, weights, out, slabs, lhs0, lhs1, rhs0, rhs1, low0, low1, sems):
    i = pl.program_id(0)
    pair = ((lhs0, rhs0, low0), (lhs1, rhs1, low1))

    def load(n):
        return pltpu.make_async_copy(slabs_hbm.at[n], slabs.at[n], sems.at[n])

    low = lax.broadcasted_iota(jnp.int32, (8, W), 0) < RB
    lane = lax.broadcasted_iota(jnp.int32, (8, 128), 1)[None]
    second = (lane >= 64) & (lane < 80)
    third = (lane >= 32) & (lane < 48)

    def prepare(c, lhs, rhs, low_rhs):
        here = pl.ds(pl.multiple_of(c * W, W), W)
        rel = offsets[:, here] - c * W
        wts = weights[:, here]

        def coefficients(row, cols):
            ahead = row - rel[:, cols]
            total = jnp.zeros(ahead.shape, F32)
            for k in range(BW):
                total = jnp.where(ahead == k, wts[k : k + 1, cols], total)
            return halves(total)

        for start, cols in ((0, slice(0, 128)), (112, slice(128, 256))):
            high, small = coefficients(start + lax.broadcasted_iota(jnp.int32, (144, 128), 0), cols)
            rhs[start : start + 144, cols] = high
            rhs[W + start : W + start + 144, cols] = high
            low_rhs[start : start + 144, cols] = small
        row = lax.broadcasted_iota(jnp.int32, (16, W), 0)
        high, small = coefficients(jnp.where(row < 8, row - 8, row + (W - 8)), slice(0, W))
        high32 = high.astype(F32)
        none = jnp.zeros((8, W), F32)
        rhs[2 * W : 2 * W + 16, :] = jnp.concatenate([high32[8:], none], axis=0).astype(BF16)
        rhs[2 * W + 32 : 2 * W + 48, :] = small
        rhs[2 * W + 64 : 2 * W + 80, :] = high
        rhs[2 * W + 112 : 2 * W + 128, :] = jnp.concatenate([none, high32[:8]], axis=0).astype(BF16)

        before = jnp.maximum(c - 1, 0)
        after = jnp.minimum(c + 1, NDET - 1)

        def gain(chunk, j):
            tile = gains[j // 2, chunk]
            turned = pltpu.roll(tile, RB, 0)
            return jnp.where(low, tile, turned) if j % 2 == 0 else jnp.where(low, turned, tile)

        for j in range(MOST):
            g = gain(c, j)[None]
            ge = jnp.where(lane >= 64, gain(before, j)[None, :, 128:], gain(after, j)[None, :, :128])
            for h in range(2):
                rows = slice((h * MOST + j) * 64, (h * MOST + j) * 64 + 64)
                a, b = halves((slabs[c, h, j] - g).reshape(64, W))
                lhs[rows, 0:W] = a
                lhs[rows, W : 2 * W] = b
                e = jnp.where(lane >= 64, slabs[before, h, j, :, :, 128:], slabs[after, h, j, :, :, :128]) - ge
                e = jnp.where(second, pltpu.roll(e, 72, 2), jnp.where(third, pltpu.roll(e, 40, 2), e))
                high = e.astype(BF16).astype(F32)
                lhs[rows, 2 * W :] = jnp.where(second, e - high, e).reshape(64, 128).astype(BF16)

    def product(side, lhs, rhs, low_rhs):
        acc = jnp.dot(lhs[...], rhs[...], preferred_element_type=F32)
        acc = acc + jnp.dot(lhs[:, 0:W], low_rhs[...], preferred_element_type=F32)
        for h in range(2):
            for j in range(MOST):
                rows = slice((h * MOST + j) * 64, (h * MOST + j) * 64 + 64)
                out[16 * h : 16 * h + 16, j, :, side * W : side * W + W] = acc[rows].reshape(16, RB, W)

    @pl.when(i == 0)
    def _():
        for n in range(8):
            load(n).start()

        for _, rhs, low_rhs in pair:
            rhs[...] = jnp.zeros(rhs.shape, BF16)
            low_rhs[...] = jnp.zeros(low_rhs.shape, BF16)
        load(0).wait()
        load(1).wait()
        prepare(0, *pair[0])

    @pl.when(i < NDET // 2 - 4)
    def _():
        load(2 * i + 8).start()
        load(2 * i + 9).start()

    @pl.when(i < NDET // 2 - 1)
    def _():
        load(2 * i + 2).wait()
        load(2 * i + 3).wait()

    prepare(2 * i + 1, *pair[1])
    product(0, *pair[0])
    prepare(jnp.minimum(2 * i + 2, NDET - 1), *pair[0])
    product(1, *pair[1])


def rebin(slabs, gains, offsets, weights):
    return pl.pallas_call(
        rebin_kernel,
        grid=(NDET // 2,),
        out_shape=pltpu.HBM((32, MOST, RB, COLS), F32),
        in_specs=[
            pl.BlockSpec(memory_space=pl.ANY),
            pl.BlockSpec((2, NDET, 8, W), lambda c: (0, 0, 0, 0)),
            pl.BlockSpec((1, COLS), lambda c: (0, 0)),
            pl.BlockSpec((BW, COLS), lambda c: (0, 0)),
        ],
        out_specs=pl.BlockSpec((32, MOST, RB, 2 * W), lambda c: (0, 0, 0, c)),
        scratch_shapes=[pltpu.VMEM((NDET, 2, MOST, 8, 8, W), F32)]
        + [pltpu.VMEM((512, 2 * W + 128), BF16)] * 2
        + [pltpu.VMEM((2 * W + 128, W), BF16)] * 2
        + [pltpu.VMEM((W, W), BF16)] * 2
        + [pltpu.SemaphoreType.DMA((NDET,))],
        compiler_params=pltpu.CompilerParams(vmem_limit_bytes=24 * 2**20),
        name="rebin",
    )(slabs, gains, offsets.reshape(1, COLS), weights)


def body(raw_counts, dark_field, flat_field, destinations, band_offsets, band_weights):
    plan, branch = make_plan(destinations)

    def with_cap(cap):
        def both(plan, raw, dark, flat, offsets, weights):
            slabs, gains = move(cap, plan, raw, dark, flat)
            return rebin(slabs, gains, offsets, weights)

        return both

    return lax.switch(
        branch[0],
        [with_cap(cap) for cap in CAPS],
        plan, raw_counts, dark_field, flat_field, band_offsets, band_weights,
    )


def solution(mesh):
    placed = (P("ang", None, "det"), P(None, "det"), P(None, "det"), P(), P(), P())
    return jax.shard_map(
        body, mesh=mesh, in_specs=placed, out_specs=P("ang", "det", None, None), check_vma=False
    )
```
